256 devices in a mesh: seq: 32 (over x, z), head: 8 (over y, core).
Axes of the slice: x: 4, y: 4, z: 8, core: 2. Of those that a mesh axis runs over, the one named last changes fastest.
Arguments:
- tokens: bfloat16 [16384, 4096], P(('seq', 'head')), may hold values from -24 to 24
- in_weight: bfloat16 [4096, 8192], P('seq', 'head'), may hold values from -0.09375 to 0.09375
- write_proj: bfloat16 [16384, 128], P(('seq', 'head')), may hold values from -6 to 6
- read_proj: bfloat16 [16384, 128], P(('seq', 'head')), may hold values from -0.5 to 0.5
- log_decay: float32 [128, 16384], P('head', 'seq'), may hold values from -1.1 to 0, as said below
- level_gain: float32 [9, 128, 16384], P(None, 'head', 'seq'), may hold values from 0 to 1, as said below
- out_grad: bfloat16 [16384, 8192], P('seq', 'head'), may hold values from -6 to 6
Outputs:
- layer_out: bfloat16 [16384, 8192], P('seq', 'head')
- weight_grad: bfloat16 [4096, 8192], P('seq', 'head')
The draws below stay inside these ranges and needn't reach their ends.
Inputs may be any that keep to these rules, and one draw needn't show every extreme that they name: `log_decay`: Log-decays are non-positive. `level_gain`: level weights are positive.
All inputs are finite; a program needn't handle non-finite values.
Results may differ from the reference program's by a relative error of at most 0.02.
Values may be sent and summed in bfloat16 or wider, within the bound.
No kernel may reach another device: no remote copies, remote signals or barrier semaphores. Data moves between devices by JAX's collectives and lax.ppermute only.
A program may use at most 128 MiB of HBM per device.

```python
import math
import jax
import jax.numpy as jnp
from jax import lax

D = 4096
HEAD_COUNT = 128
HEAD_DIM = 64
STATE = 128
CH = 64
TOK_DEV = 512
TOKEN_COUNT = 16384
LOCAL_LEVELS = 4
SEQ_LEVELS = 5
LEVELS = 9
N_SEQ = 32


def draw_log_decay(key, part):
    random_keys = jax.random.split(key, 7)
    fast_share = 0.5
    rough_low = 0.5
    rough_high = 1.5
    is_fast = jax.random.uniform(random_keys[0], (HEAD_COUNT,)) < fast_share
    fast_rate = jax.random.uniform(random_keys[1], (HEAD_COUNT,), minval=1.0 / 50.0, maxval=1.0 / 30.0)
    slow_rate = jnp.exp(jax.random.uniform(random_keys[2], (HEAD_COUNT,), minval=math.log(0.03), maxval=math.log(0.4))) / TOKEN_COUNT
    decay_speed = jnp.where(is_fast, fast_rate, slow_rate)
    segment_count = TOKEN_COUNT // TOK_DEV
    multiplier = jax.random.uniform(random_keys[3], (HEAD_COUNT, segment_count), minval=0.5, maxval=1.5)
    multiplier = jnp.repeat(multiplier, TOK_DEV, axis=1)
    jaggedness = jax.random.uniform(random_keys[4], (HEAD_COUNT, TOKEN_COUNT), minval=rough_low, maxval=rough_high)
    spike_position = jax.random.randint(random_keys[5], (HEAD_COUNT, 2, 1), 0, TOKEN_COUNT)
    spike_loss = jnp.log(jax.random.uniform(random_keys[6], (HEAD_COUNT, 2, 1), minval=0.6, maxval=0.8))
    token_position = jnp.arange(TOKEN_COUNT, dtype=jnp.int32)[None, None, :]
    spike_events = jnp.sum(jnp.where(token_position == spike_position, spike_loss, 0.0), axis=1)
    return (-decay_speed[:, None] * multiplier * jaggedness + spike_events).astype(jnp.float32)


def draw_level_gain(key, part):
    number = jnp.arange(LEVELS)
    level_span = CH * jnp.exp2(jnp.maximum(number - 1, 0).astype(jnp.float32))
    jaggedness = jax.random.uniform(key, (LEVELS, HEAD_COUNT, TOKEN_COUNT), minval=0.3, maxval=1.2)
    return (jaggedness / jnp.sqrt(level_span)[:, None, None]).astype(jnp.float32)


def raised(values, own_key, source, target, shards_of, factor):
    def block_of(axis_at):
        return (jnp.arange(values.shape[axis_at]) // (values.shape[axis_at] // shards_of)).reshape((-1,) + (1,) * (values.ndim - 1 - axis_at))

    one_side = jax.random.permutation(own_key, shards_of)[block_of(target)]
    other_side = (block_of(target) + shards_of // 2) % shards_of
    return jnp.where((block_of(source) == one_side) | (block_of(source) == other_side), factor * values, values)


def block_levels(rng, dims, cuts, least, top_value):
    level, own = 1.0, jax.random.fold_in(rng, 6)
    for axis_at, parts in cuts:
        draws = jnp.exp(jax.random.uniform(jax.random.fold_in(own, axis_at), (parts,), jnp.float32, least / len(cuts), top_value / len(cuts)))
        level = level * jnp.repeat(draws, dims[axis_at] // parts).reshape([-1 if axis == axis_at else 1 for axis in range(len(dims))])
    return level


def noise(rng, dims, spread, limit, cuts=(), kind=jnp.bfloat16):
    level = block_levels(rng, dims, cuts, -0.22, 0.18) if cuts else 1.0
    entries = jax.random.normal(rng, dims, jnp.float32) * spread * level
    return jnp.minimum(jnp.maximum(entries, -limit), limit).astype(kind)


def heavy_noise(key, shape, width, bound, cuts, heavy, kind=jnp.bfloat16):
    drawn = width * jax.random.normal(key, shape, jnp.float32)
    if cuts:
        drawn = drawn * block_levels(key, shape, cuts, -0.22, 0.18)
    return jnp.clip(raised(drawn, jax.random.fold_in(key, 3), *heavy), -bound, bound).astype(kind)


def setup_inputs(seed: int = 0) -> dict:
    keys = jax.random.split(jax.random.key(seed), 8)
    tokens = heavy_noise(keys[0], (TOKEN_COUNT, D), 1.0, 24.0, ((0, 256),), (0, 1, 256, 6.0))
    in_weight = noise(keys[1], (D, HEAD_COUNT * HEAD_DIM), D ** -0.5, 0.09375, ((0, 32), (1, 8)))
    write_proj = noise(keys[2], (TOKEN_COUNT, STATE), 1.0, 6.0, ((0, 256),))
    read_proj = noise(keys[3], (TOKEN_COUNT, STATE), STATE ** -0.5, 0.5, ((0, 256),))
    log_decay = draw_log_decay(jax.random.fold_in(keys[7], 71), 0)
    level_gain = draw_level_gain(jax.random.fold_in(keys[7], 71), 0)
    out_grad = noise(keys[6], (TOKEN_COUNT, HEAD_COUNT * HEAD_DIM), 1.0, 6.0, ((0, 32), (1, 8)))
    return dict(tokens=tokens, in_weight=in_weight, write_proj=write_proj, read_proj=read_proj, log_decay=log_decay, level_gain=level_gain, out_grad=out_grad)


def stretch_levels(length, level_count):
    stretches = jnp.arange(length, dtype=jnp.int32) // CH
    level_table = jnp.zeros((length, length), jnp.int32)
    for offset in range(level_count - 1):
        level_table = level_table + ((stretches[:, None] >> offset) != (stretches[None, :] >> offset)).astype(jnp.int32)
    return level_table


def head_terms(scores, level_table, causal, cumulative, gain_rows, values, grad_rows):
    gain_table = jnp.zeros(scores.shape, jnp.float32)
    for number in range(gain_rows.shape[0]):
        gain_table = gain_table + jnp.where(level_table == number, gain_rows[number][:, None], 0.0)
    differ = cumulative[:, None] - cumulative[None, :]
    decays = jnp.where(causal, jnp.exp(jnp.where(causal, differ, 0.0)), 0.0)
    weights = (gain_table * decays * scores).astype(jnp.bfloat16)
    forward = jnp.dot(weights, values, preferred_element_type=jnp.float32)
    backward = lax.dot_general(weights, grad_rows, (((0,), (0,)), ((), ())), preferred_element_type=jnp.float32)
    return forward, backward


def level_of(seg_index, order):
    differing = jnp.zeros(order.shape, jnp.int32)
    for offset in range(SEQ_LEVELS):
        differing = differing + ((seg_index >> offset) != (order >> offset)).astype(jnp.int32)
    return differing - 1


def make_keys(cumulative, totals, write_rows):
    scale_rows = jnp.exp(totals[:, None] - cumulative)
    return (scale_rows[:, :, None] * write_rows.astype(jnp.float32)[None]).astype(jnp.bfloat16)


def make_queries(cumulative, gain_rows, read_rows):
    scale_rows = gain_rows[LOCAL_LEVELS:] * jnp.exp(cumulative)[None]
    return (scale_rows[..., None] * read_rows.astype(jnp.float32)[None, None]).astype(jnp.bfloat16)


def to_half(array):
    return lax.optimization_barrier(array.astype(jnp.bfloat16)).astype(jnp.float32)


def reference(tokens, in_weight, write_proj, read_proj, log_decay, level_gain, out_grad):
    segments = N_SEQ
    inner_width = HEAD_COUNT * HEAD_DIM
    highest = lax.Precision.HIGHEST
    values = jnp.dot(tokens, in_weight, preferred_element_type=jnp.float32).astype(jnp.bfloat16)
    values_seg = values.reshape(segments, TOK_DEV, HEAD_COUNT, HEAD_DIM)
    tokens_seg = tokens.reshape(segments, TOK_DEV, D)
    write_seg = write_proj.reshape(segments, TOK_DEV, STATE)
    read_seg = read_proj.reshape(segments, TOK_DEV, STATE)
    cumulative = jnp.cumsum(log_decay.reshape(HEAD_COUNT, segments, TOK_DEV), axis=2).transpose(1, 0, 2)
    totals = cumulative[:, :, -1]
    gains_seg = level_gain.reshape(LEVELS, HEAD_COUNT, segments, TOK_DEV).transpose(2, 0, 1, 3)
    grads_seg = out_grad.reshape(segments, TOK_DEV, HEAD_COUNT, HEAD_DIM)

    def summarize(inputs):
        cum_rows, total_rows, write_rows, read_rows, value_rows, gain_rows, grad_rows = inputs
        key_rows = make_keys(cum_rows, total_rows, write_rows)
        seg_state = jnp.einsum('htn,thp->hnp', key_rows.astype(jnp.float32), value_rows.astype(jnp.float32), precision=highest)
        queries = make_queries(cum_rows, gain_rows, read_rows)
        level_grad = jnp.einsum('bhtn,thp->bhnp', queries.astype(jnp.float32), grad_rows.astype(jnp.float32), precision=highest)
        return seg_state, level_grad

    states, level_grads = lax.map(summarize, (cumulative, totals, write_seg, read_seg, values_seg, gains_seg, grads_seg))
    running = jnp.cumsum(totals, axis=0)
    before = running - totals
    order = jnp.arange(segments, dtype=jnp.int32)
    level_table = stretch_levels(TOK_DEV, LOCAL_LEVELS)
    steps_idx = jnp.arange(TOK_DEV, dtype=jnp.int32)
    causal = steps_idx[:, None] >= steps_idx[None, :]

    def segment_step(accumulated, inputs):
        seg_index, cum_rows, total_rows, write_rows, read_rows, value_rows, gain_rows, grad_rows, token_rows = inputs
        levels_seg = level_of(seg_index, order)
        is_earlier = (order < seg_index)[:, None]
        is_later = (order > seg_index)[:, None]
        to_here = jnp.where(is_earlier, jnp.exp(jnp.where(is_earlier, before[seg_index][None, :] - running, 0.0)), 0.0)
        from_here = jnp.where(is_later, jnp.exp(jnp.where(is_later, before - running[seg_index][None, :], 0.0)), 0.0)
        onehot = (levels_seg[None, :] == jnp.arange(SEQ_LEVELS, dtype=jnp.int32)[:, None]).astype(jnp.float32)
        buckets = jnp.einsum('bj,jh,jhnp->bhnp', onehot, to_here, states, precision=highest)
        state_grad = jnp.einsum('bk,kh,kbhnp->hnp', onehot, from_here, level_grads, precision=highest)
        bucket_half = to_half(buckets)
        state_half = to_half(state_grad)
        queries = make_queries(cum_rows, gain_rows, read_rows)
        cross_term = jnp.einsum('bhtn,bhnp->thp', queries.astype(jnp.float32), bucket_half, precision=highest)
        key_rows = make_keys(cum_rows, total_rows, write_rows)
        cross_grad = jnp.einsum('htn,hnp->thp', key_rows.astype(jnp.float32), state_half, precision=highest)
        scores = lax.dot_general(read_rows, write_rows, (((1,), (1,)), ((), ())), preferred_element_type=jnp.float32)

        def one_head(packed):
            cum_head, gain_head, value_head, grad_head = packed
            return head_terms(scores, level_table, causal, cum_head, gain_head, value_head, grad_head)

        local_out, local_grad = lax.map(one_head, (cum_rows, gain_rows[:LOCAL_LEVELS].transpose(1, 0, 2), value_rows.transpose(1, 0, 2), grad_rows.transpose(1, 0, 2)))
        layer_seg = (cross_term + local_out.transpose(1, 0, 2)).astype(jnp.bfloat16).reshape(TOK_DEV, inner_width)
        values_grad = (cross_grad + local_grad.transpose(1, 0, 2)).astype(jnp.bfloat16).reshape(TOK_DEV, inner_width)
        partial_grad = lax.dot_general(token_rows, values_grad, (((0,), (0,)), ((), ())), preferred_element_type=jnp.float32).astype(jnp.bfloat16)
        return accumulated + partial_grad.astype(jnp.float32), layer_seg

    start_sum = jnp.zeros((D, inner_width), jnp.float32)
    accumulated, layers = lax.scan(segment_step, start_sum, (order, cumulative, totals, write_seg, read_seg, values_seg, gains_seg, grads_seg, tokens_seg))
    return layers.reshape(TOKEN_COUNT, inner_width), accumulated.astype(jnp.bfloat16)
```

```python
import jax
import jax.numpy as jnp
from jax import lax
from jax.experimental import pallas as pl
from jax.experimental.pallas import tpu as pltpu
from jax.sharding import Mesh
from jax.sharding import PartitionSpec as P

HEAD_DIM = 64
STATE = 128
TOK = 512
CH = 64
NZ = 8
NX = 4
PAIR = 2 * HEAD_DIM
LOCAL = 4
SEQ = ("seq_0", "seq_1")
SEQ_HEAD = ("seq_0", "seq_1", "head")
F32 = jnp.float32
BF16 = jnp.bfloat16
C_BWD, C_FWD, C_START, C_END, C_LATER, C_EARLIER = 0, 128, 256, 272, 288, 304

NT = (((1,), (1,)), ((), ()))
NN = (((1,), (0,)), ((), ()))


def dot(a, b, dims=NN):
    return lax.dot_general(a, b, dims, preferred_element_type=F32)


def spread(rows, each=HEAD_DIM):
    n, t = rows.shape
    return jnp.concatenate([jnp.broadcast_to(rows[i : i + 1], (each, t)) for i in range(n)], axis=0)


def owner_of(slot_base, slot):
    return (slot_base + slot) & (NZ - 1)


def columns(ref, pair):
    return ref[:, pl.ds(pl.multiple_of(pair * PAIR, PAIR), PAIR)]


def rows_at(ref, pair):
    return ref[pl.ds(pl.multiple_of(pair * PAIR, PAIR), PAIR), :]


def vmem():
    return pl.BlockSpec(memory_space=pltpu.VMEM)


def smem():
    return pl.BlockSpec(memory_space=pltpu.SMEM)


def call(kernel, name, outs, n_smem, n_vmem, scratch=(), flops=0):
    return pl.pallas_call(
        kernel,
        name=name,
        out_shape=outs,
        in_specs=[smem()] * n_smem + [vmem()] * n_vmem,
        out_specs=[vmem() for _ in outs],
        scratch_shapes=scratch,
        compiler_params=pltpu.CompilerParams(vmem_limit_bytes=48 << 20),
    )


def shaped(shape, dtype):
    return jax.ShapeDtypeStruct(shape, dtype)


def level_grad_kernel(place, grad, read, cum, gain, *outs):
    z = place[1]
    read_rows = read[...]
    for slot in range(NZ):
        pair = owner_of(z, slot)
        rows = columns(grad, pair).astype(F32).T
        decay = jnp.exp(cum[pair])
        for b in range(5):
            scaled = (rows * spread(gain[LOCAL + b, pair] * decay)).astype(BF16)
            outs[slot][b] = dot(scaled, read_rows).astype(BF16)


def state_kernel(place, values, write, cum, *outs):
    z = place[1]
    write_rows = write[...]
    for slot in range(NZ):
        pair = owner_of(z, slot)
        rows = columns(values, pair).astype(F32).T
        c = cum[pair]
        scaled = (rows * spread(jnp.exp(c[:, TOK - 1 :] - c))).astype(BF16)
        outs[slot][...] = dot(scaled, write_rows).astype(BF16)


def local_kernel(forward, source, read, write, cum, gain, out, score_ref):
    score_ref[...] = dot(write[...], read[...], NT)
    half = score_ref[...].astype(BF16)
    row_id = lax.broadcasted_iota(jnp.int32, (128, 128), 0)
    col_id = lax.broadcasted_iota(jnp.int32, (128, 128), 1)
    causal = row_id <= col_id
    crosses = (row_id < CH) & (col_id >= CH)

    def one_pair(pair, carry):
        rows = columns(source, pair).T
        rows_f = rows.astype(F32)
        c = cum[pair]
        c_col = jnp.concatenate([c, jnp.zeros((6, TOK), F32)], axis=0).T
        g0, g1, g2, g3 = (gain[level, pair] for level in range(LOCAL))

        def far(lo, mid, hi, g):
            edge = c[:, mid - 1 : mid]
            before = spread(jnp.exp(edge - c[:, lo:mid]))
            after = spread(g[:, mid:hi] * jnp.exp(c[:, mid:hi] - edge))
            block = half[lo:mid, mid:hi]
            if forward:
                return dot((rows_f[:, lo:mid] * before).astype(BF16), block) * after
            return dot((rows_f[:, mid:hi] * after).astype(BF16), block, NT) * before

        near = []
        for i in range(4):
            lo, hi = i * 128, i * 128 + 128
            score = score_ref[lo:hi, lo:hi]
            parts = []
            for h in range(2):
                differ = c[h : h + 1, lo:hi] - c_col[lo:hi, h : h + 1]
                decays = jnp.exp(jnp.where(causal, differ, -1e30))
                gains = jnp.where(crosses, g1[h : h + 1, lo:hi], g0[h : h + 1, lo:hi])
                weights = (gains * decays * score).astype(BF16)
                parts.append(
                    dot(rows[h * HEAD_DIM : (h + 1) * HEAD_DIM, lo:hi], weights, NN if forward else NT)
                )
            near.append(jnp.concatenate(parts, axis=0))
        wide = far(0, 256, 512, g3)
        left, right = far(0, 128, 256, g2), far(256, 384, 512, g2)
        if forward:
            near[1] += left
            near[3] += right
            near[2] += wide[:, :128]
            near[3] += wide[:, 128:]
        else:
            near[0] += left
            near[2] += right
            near[0] += wide[:, :128]
            near[1] += wide[:, 128:]
        at = pl.ds(pl.multiple_of(pair * PAIR, PAIR), PAIR)
        for i in range(4):
            out[at, i * 128 : i * 128 + 128] = near[i]
        return carry

    lax.fori_loop(0, NZ, one_pair, 0)


def by_head(fn):
    return jnp.concatenate([fn(0), fn(1)], axis=0)


def weighted(coef, base, value):
    return jnp.concatenate(
        [value[:HEAD_DIM] * coef[base], value[HEAD_DIM:] * coef[base + 1]], axis=0
    )


def pair_at(coef, offset, index, span):
    return (coef[offset + index], coef[offset + span + index])


def scaled_pair(two, value):
    return jnp.concatenate([value[:HEAD_DIM] * two[0], value[HEAD_DIM:] * two[1]], axis=0)


def later_sum_kernel(place, coef, *refs):
    z = place[1]
    pieces, out = refs[:NZ], refs[NZ]
    for b in range(2):
        total = jnp.zeros((PAIR, STATE), F32)
        for slot in range(NZ):
            source = (z - slot) & (NZ - 1)
            total += scaled_pair(pair_at(coef, C_START, source, 8), pieces[slot][3 + b].astype(F32))
        out[b] = total.astype(BF16)


def state_grad_kernel(place, coef, level, *refs):
    x, z = place[0], place[1]
    pieces, others, outs = refs[:NZ], refs[NZ : NZ + 3], refs[NZ + 3 :]
    later = jnp.zeros((PAIR, STATE), F32)
    for k in range(1, NX):
        source = (x - k) & (NX - 1)
        for b in range(2):
            two = pair_at(coef, C_LATER, source * 2 + b, 8)
            later += scaled_pair(two, others[k - 1][b].astype(F32))
    for slot in range(NZ):
        target = (z + slot) & (NZ - 1)
        total = scaled_pair(pair_at(coef, C_END, target, 8), later)
        for back in range(NZ):
            source = (z - back) & (NZ - 1)
            two = pair_at(coef, C_BWD, source * 8 + target, 64)
            total += scaled_pair(two, pieces[back][level[source * 8 + target]].astype(F32))
        outs[slot][...] = total.astype(BF16)


def block_sum_kernel(place, coef, *refs):
    z = place[1]
    pieces, out = refs[:NZ], refs[NZ]
    total = jnp.zeros((PAIR, STATE), F32)
    for slot in range(NZ):
        source = (z - slot) & (NZ - 1)
        total += scaled_pair(pair_at(coef, C_END, source, 8), pieces[slot][...].astype(F32))
    out[...] = total.astype(BF16)


def bucket_kernel(place, coef, level, *refs):
    x, z = place[0], place[1]
    pieces, others, outs = refs[:NZ], refs[NZ : NZ + 3], refs[NZ + 3 : NZ + 3 + NZ]
    scratch = refs[NZ + 3 + NZ]
    earlier = []
    for b in range(2):
        total = jnp.zeros((PAIR, STATE), F32)
        for k in range(1, NX):
            source = (x - k) & (NX - 1)
            two = pair_at(coef, C_EARLIER, source * 2 + b, 8)
            total += scaled_pair(two, others[k - 1][...].astype(F32))
        earlier.append(total)
    for slot in range(NZ):
        target = (z + slot) & (NZ - 1)
        for b in range(3):
            scratch[b] = jnp.zeros((PAIR, STATE), F32)
        for back in range(NZ):
            source = (z - back) & (NZ - 1)
            two = pair_at(coef, C_FWD, source * 8 + target, 64)
            at = level[source * 8 + target]
            scratch[at] = scratch[at] + scaled_pair(two, pieces[back][...].astype(F32))
        for b in range(3):
            outs[slot][b] = scratch[b].astype(BF16)
        for b in range(2):
            outs[slot][3 + b] = scaled_pair(
                pair_at(coef, C_START, target, 8), earlier[b]
            ).astype(BF16)


def values_grad_kernel(place, local, write, cum, *refs):
    z = place[1]
    states, out = refs[:NZ], refs[NZ]
    write_rows = write[...]
    for slot in range(NZ):
        pair = (z - slot) & (NZ - 1)
        c = cum[pair]
        rows = dot(states[slot][...], write_rows, NT) * spread(jnp.exp(c[:, TOK - 1 :] - c))
        rows += rows_at(local, pair)
        out[:, pl.ds(pl.multiple_of(pair * PAIR, PAIR), PAIR)] = rows.T.astype(BF16)


def layer_out_kernel(place, local, read, cum, gain, *refs):
    z = place[1]
    buckets, out = refs[:NZ], refs[NZ]
    read_rows = read[...]
    for slot in range(NZ):
        pair = (z - slot) & (NZ - 1)
        decay = jnp.exp(cum[pair])
        rows = rows_at(local, pair)
        for b in range(5):
            rows += dot(buckets[slot][b], read_rows, NT) * spread(gain[LOCAL + b, pair] * decay)
        out[:, pl.ds(pl.multiple_of(pair * PAIR, PAIR), PAIR)] = rows.T.astype(BF16)


def shift(value, axis, apart):
    size = lax.axis_size(axis)
    return lax.ppermute(value, axis, [(i, (i + apart) % size) for i in range(size)])


def deal(pieces):
    return [pieces[0]] + [shift(pieces[d], "seq_1", d) for d in range(1, NZ)]


def around_x(value):
    return [shift(value, "seq_0", k) for k in range(1, NX)]


def coefficients(totals, x, z):
    mine = lax.dynamic_slice_in_dim(totals, 2 * z, 2, axis=1).T
    upto = jnp.cumsum(mine, axis=1)
    before = upto - mine
    upto4, before4 = upto.reshape(2, NX, NZ), before.reshape(2, NX, NZ)
    upto_x = lax.dynamic_index_in_dim(upto4, x, 1, keepdims=False)
    before_x = lax.dynamic_index_in_dim(before4, x, 1, keepdims=False)
    order = jnp.arange(NZ)
    source, target = order[:, None], order[None, :]

    def decayed(keep, value):
        return jnp.where(keep, jnp.exp(jnp.where(keep, value, 0.0)), 0.0)

    bwd = decayed(source > target, before_x[:, :, None] - upto_x[:, None, :])
    fwd = decayed(source < target, before_x[:, None, :] - upto_x[:, :, None])
    start = jnp.exp(before_x - before_x[:, :1])
    end = jnp.exp(upto_x[:, -1:] - upto_x)
    blocks = jnp.arange(NX)[:, None]
    top = (blocks >> 1 != x >> 1).astype(jnp.int32)
    is_level = top == jnp.arange(2)[None, :]
    later = decayed(
        (blocks > x) & is_level, (before4[:, :, 0] - upto_x[:, -1:])[:, :, None]
    )
    earlier = decayed(
        (blocks < x) & is_level, (before_x[:, :1] - upto4[:, :, -1])[:, :, None]
    )
    parts = (bwd, fwd, start, end, later, earlier)
    return jnp.concatenate([part.reshape(-1) for part in parts])


def per_device(tokens, in_weight, write_proj, read_proj, log_decay, level_gain, out_grad):
    x, z = lax.axis_index("seq_0"), lax.axis_index("seq_1")
    place = jnp.stack([x, z]).astype(jnp.int32)
    both = lax.all_gather(
        jnp.concatenate([write_proj, read_proj], axis=1), "head", axis=0, tiled=True
    )
    write, read = both[:, :STATE], both[:, STATE:]
    full_tokens = lax.all_gather(tokens, "head", axis=0, tiled=True)
    cumulative = jnp.cumsum(log_decay, axis=1)
    totals = lax.all_gather(cumulative[:, -1], SEQ, axis=0, tiled=False)
    weight = lax.all_gather(in_weight, SEQ, axis=0, tiled=True)
    cum = cumulative.reshape(NZ, 2, TOK)
    gain = level_gain.reshape(LOCAL + 5, NZ, 2, TOK)
    coef = coefficients(totals, x, z)
    order = jnp.arange(NZ, dtype=jnp.int32)
    mixed = order[:, None] ^ order[None, :]
    level = ((mixed > 1).astype(jnp.int32) + (mixed > 3)).reshape(-1)

    piece5, piece = shaped((5, PAIR, STATE), BF16), shaped((PAIR, STATE), BF16)
    rows = shaped((NZ * PAIR, TOK), F32)
    natural = shaped((TOK, NZ * PAIR), BF16)

    def local(source, forward, name):
        kernel = lambda *refs: local_kernel(forward, *refs)
        return call(kernel, name, [rows], 0, 5, [pltpu.VMEM((TOK, TOK), F32)])(
            source, read, write, cum, gain
        )[0]

    sent = call(level_grad_kernel, "level_grad", [piece5] * NZ, 1, 4)(
        place, out_grad, read, cum, gain
    )
    got = deal(sent)
    later = call(later_sum_kernel, "later_sum", [shaped((2, PAIR, STATE), BF16)], 2, NZ)(
        place, coef, *got
    )[0]
    grads = call(state_grad_kernel, "state_grad", [piece] * NZ, 3, NZ + 3)(
        place, coef, level, *got, *around_x(later)
    )
    local_grad = local(out_grad, False, "local_bwd")
    values_grad = call(values_grad_kernel, "values_grad", [natural], 1, 3 + NZ)(
        place, local_grad, write, cum, *deal(grads)
    )[0]
    held_tokens, weight = lax.optimization_barrier((full_tokens, weight))
    partial = lax.dot_general(
        held_tokens, values_grad, (((0,), (0,)), ((), ())), preferred_element_type=F32
    ).astype(BF16)
    weight_grad = lax.psum_scatter(partial, "seq_0", scatter_dimension=0, tiled=True)

    values = jnp.dot(full_tokens, weight, preferred_element_type=F32).astype(BF16)
    states = call(state_kernel, "seg_state", [piece] * NZ, 1, 3)(place, values, write, cum)
    got = deal(states)
    block = call(block_sum_kernel, "block_sum", [piece], 2, NZ)(place, coef, *got)[0]
    buckets = call(
        bucket_kernel, "bucket", [piece5] * NZ, 3, NZ + 3, [pltpu.VMEM((3, PAIR, STATE), F32)]
    )(place, coef, level, *got, *around_x(block))
    local_out = local(values, True, "local_fwd")
    layer_out = call(layer_out_kernel, "layer_out", [natural], 1, 4 + NZ)(
        place, local_out, read, cum, gain, *deal(buckets)
    )[0]
    weight_grad, layer_out = lax.optimization_barrier((weight_grad, layer_out))
    weight_grad = lax.psum_scatter(weight_grad, "seq_1", scatter_dimension=0, tiled=True)
    return (layer_out, weight_grad)


def solution(mesh):
    split = Mesh(mesh.devices.reshape(NX, NZ, mesh.shape["head"]), ("seq_0", "seq_1", "head"))
    in_specs = (
        P(SEQ_HEAD, None),
        P(SEQ, "head"),
        P(SEQ_HEAD, None),
        P(SEQ_HEAD, None),
        P("head", SEQ),
        P(None, "head", SEQ),
        P(SEQ, "head"),
    )
    out_specs = (P(SEQ, "head"), P(SEQ, "head"))
    return jax.shard_map(
        per_device, mesh=split, in_specs=in_specs, out_specs=out_specs, check_vma=False
    )
```

```python
import jax
import jax.numpy as jnp
from jax import lax
from jax.experimental import pallas as pl
from jax.experimental.pallas import tpu as pltpu
from jax.sharding import Mesh
from jax.sharding import PartitionSpec as P

HEAD_DIM = 64
STATE = 128
TOK = 512
CH = 64
NZ = 8
NX = 4
PAIR = 2 * HEAD_DIM
LOCAL = 4
SEQ = ("seq_0", "seq_1")
SEQ_HEAD = ("seq_0", "seq_1", "head")
F32 = jnp.float32
BF16 = jnp.bfloat16

NT = (((1,), (1,)), ((), ()))
NN = (((1,), (0,)), ((), ()))


def dot(a, b, dims=NN):
    return lax.dot_general(a, b, dims, preferred_element_type=F32)


def spread(rows, each=HEAD_DIM):
    n, t = rows.shape
    return jnp.concatenate([jnp.broadcast_to(rows[i : i + 1], (each, t)) for i in range(n)], axis=0)


def owner_of(slot_base, slot):
    return (slot_base + slot) & (NZ - 1)


def columns(ref, pair):
    return ref[:, pl.ds(pl.multiple_of(pair * PAIR, PAIR), PAIR)]


def rows_at(ref, pair):
    return ref[pl.ds(pl.multiple_of(pair * PAIR, PAIR), PAIR), :]


def vmem():
    return pl.BlockSpec(memory_space=pltpu.VMEM)


def smem():
    return pl.BlockSpec(memory_space=pltpu.SMEM)


def call(kernel, name, outs, n_smem, n_vmem, scratch=(), flops=0):
    return pl.pallas_call(
        kernel,
        name=name,
        out_shape=outs,
        in_specs=[smem()] * n_smem + [vmem()] * n_vmem,
        out_specs=[vmem() for _ in outs],
        scratch_shapes=scratch,
        compiler_params=pltpu.CompilerParams(vmem_limit_bytes=48 << 20),
    )


def shaped(shape, dtype):
    return jax.ShapeDtypeStruct(shape, dtype)


def split_totals(totals):
    wide = jnp.broadcast_to(totals, (2, STATE))
    high = wide.astype(BF16).astype(F32)
    rest = wide - high
    middle = rest.astype(BF16).astype(F32)
    rows = [high, middle, rest - middle, jnp.zeros((10, STATE), F32)]
    return jnp.concatenate(rows, axis=0).astype(BF16)


def joined_totals(rows):
    rows = rows.astype(F32)
    return rows[0:2] + rows[2:4] + rows[4:6]


def level_grad_kernel(place, grad, read, cum, gain, *outs):
    z = place[1]
    read_rows = read[...]
    for slot in range(NZ):
        pair = owner_of(z, slot)
        rows = columns(grad, pair).astype(F32).T
        c = cum[pair]
        decay = jnp.exp(c)
        for b in range(5):
            scaled = (rows * spread(gain[LOCAL + b, pair] * decay)).astype(BF16)
            outs[slot][b * PAIR : (b + 1) * PAIR, :] = dot(scaled, read_rows).astype(BF16)
        outs[slot][5 * PAIR :, :] = split_totals(c[:, TOK - 1 :])


def state_kernel(place, values, write, cum, *outs):
    z = place[1]
    write_rows = write[...]
    for slot in range(NZ):
        pair = owner_of(z, slot)
        rows = columns(values, pair).astype(F32).T
        c = cum[pair]
        scaled = (rows * spread(jnp.exp(c[:, TOK - 1 :] - c))).astype(BF16)
        outs[slot][...] = dot(scaled, write_rows).astype(BF16)


def local_kernel(forward, source, read, write, cum, gain, out, score_ref):
    score_ref[...] = dot(write[...], read[...], NT)
    half = score_ref[...].astype(BF16)
    row_id = lax.broadcasted_iota(jnp.int32, (128, 128), 0)
    col_id = lax.broadcasted_iota(jnp.int32, (128, 128), 1)
    causal = row_id <= col_id
    crosses = (row_id < CH) & (col_id >= CH)

    def one_pair(pair, carry):
        rows = columns(source, pair).T
        rows_f = rows.astype(F32)
        c = cum[pair]
        c_col = jnp.concatenate([c, jnp.zeros((6, TOK), F32)], axis=0).T
        g0, g1, g2, g3 = (gain[level, pair] for level in range(LOCAL))

        def far(lo, mid, hi, g):
            edge = c[:, mid - 1 : mid]
            before = spread(jnp.exp(edge - c[:, lo:mid]))
            after = spread(g[:, mid:hi] * jnp.exp(c[:, mid:hi] - edge))
            block = half[lo:mid, mid:hi]
            if forward:
                return dot((rows_f[:, lo:mid] * before).astype(BF16), block) * after
            return dot((rows_f[:, mid:hi] * after).astype(BF16), block, NT) * before

        near = []
        for i in range(4):
            lo, hi = i * 128, i * 128 + 128
            score = score_ref[lo:hi, lo:hi]
            parts = []
            for h in range(2):
                differ = c[h : h + 1, lo:hi] - c_col[lo:hi, h : h + 1]
                decays = jnp.exp(jnp.where(causal, differ, -1e30))
                gains = jnp.where(crosses, g1[h : h + 1, lo:hi], g0[h : h + 1, lo:hi])
                weights = (gains * decays * score).astype(BF16)
                parts.append(
                    dot(rows[h * HEAD_DIM : (h + 1) * HEAD_DIM, lo:hi], weights, NN if forward else NT)
                )
            near.append(jnp.concatenate(parts, axis=0))
        wide = far(0, 256, 512, g3)
        left, right = far(0, 128, 256, g2), far(256, 384, 512, g2)
        if forward:
            near[1] += left
            near[3] += right
            near[2] += wide[:, :128]
            near[3] += wide[:, 128:]
        else:
            near[0] += left
            near[2] += right
            near[0] += wide[:, :128]
            near[1] += wide[:, 128:]
        at = pl.ds(pl.multiple_of(pair * PAIR, PAIR), PAIR)
        for i in range(4):
            out[at, i * 128 : i * 128 + 128] = near[i]
        return carry

    lax.fori_loop(0, NZ, one_pair, 0)


def between(table, upper, lower):
    return [
        jnp.exp(table[h, pl.ds(upper, 1), :] - table[h, pl.ds(lower, 1), :]) for h in range(2)
    ]


def only_if(condition, two):
    return [jnp.where(condition, one, 0.0) for one in two]


def scaled_pair(two, value):
    value = value.astype(F32)
    return jnp.concatenate([value[:HEAD_DIM] * two[0], value[HEAD_DIM:] * two[1]], axis=0)


def running_sums(table, count, scratch):
    for h in range(2):
        total = jnp.zeros((1, STATE), F32)
        for i in range(count):
            table[h, i : i + 1, :] = total
            total = total + scratch[h, i : i + 1, :]
        table[h, count : count + 1, :] = total


def later_sum_kernel(place, *refs):
    z = place[1]
    pieces, out, table, scratch = refs[:NZ], refs[NZ], refs[NZ + 1], refs[NZ + 2]
    for slot in range(NZ):
        source = (z - slot) & (NZ - 1)
        totals = joined_totals(pieces[slot][5 * PAIR :, :])
        for h in range(2):
            scratch[h, pl.ds(source, 1), :] = totals[h : h + 1]
    running_sums(table, NZ, scratch)
    starts = [between(table, (z - slot) & (NZ - 1), 0) for slot in range(NZ)]
    for b in range(2):
        total = jnp.zeros((PAIR, STATE), F32)
        for slot in range(NZ):
            total += scaled_pair(starts[slot], pieces[slot][(3 + b) * PAIR : (4 + b) * PAIR, :])
        out[b * PAIR : (b + 1) * PAIR, :] = total.astype(BF16)
    whole = jnp.concatenate([table[h, NZ : NZ + 1, :1] for h in range(2)], axis=0)
    out[2 * PAIR :, :] = split_totals(whole)


def state_grad_kernel(place, table, *refs):
    x, z = place[0], place[1]
    pieces, others, outs = refs[:NZ], refs[NZ : NZ + 3], refs[NZ + 3 : NZ + 3 + NZ]
    x_table, scratch = refs[NZ + 3 + NZ :]
    for h in range(2):
        scratch[h, pl.ds(x, 1), :] = table[h, NZ : NZ + 1, :]
    for k in range(1, NX):
        source = (x - k) & (NX - 1)
        totals = joined_totals(others[k - 1][2 * PAIR :, :])
        for h in range(2):
            scratch[h, pl.ds(source, 1), :] = totals[h : h + 1]
    running_sums(x_table, NX, scratch)
    later = jnp.zeros((PAIR, STATE), F32)
    for k in range(1, NX):
        source = (x - k) & (NX - 1)
        two = only_if(source > x, between(x_table, source, jnp.minimum(x + 1, source)))
        level = ((source ^ x) > 1).astype(jnp.int32)
        later += scaled_pair(two, rows_at(others[k - 1], level))
    for slot in range(NZ):
        target = (z + slot) & (NZ - 1)
        total = scaled_pair(between(table, NZ, target + 1), later)
        for back in range(NZ):
            source = (z - back) & (NZ - 1)
            two = only_if(source > target, between(table, source, jnp.minimum(target + 1, source)))
            mixed = source ^ target
            level = (mixed > 1).astype(jnp.int32) + (mixed > 3).astype(jnp.int32)
            total += scaled_pair(two, rows_at(pieces[back], level))
        outs[slot][...] = total.astype(BF16)


def block_sum_kernel(place, table, *refs):
    z = place[1]
    pieces, out = refs[:NZ], refs[NZ]
    total = jnp.zeros((PAIR, STATE), F32)
    for slot in range(NZ):
        source = (z - slot) & (NZ - 1)
        total += scaled_pair(between(table, NZ, source + 1), pieces[slot][...])
    out[...] = total.astype(BF16)


def bucket_kernel(place, table, x_table, *refs):
    x, z = place[0], place[1]
    pieces, others, outs = refs[:NZ], refs[NZ : NZ + 3], refs[NZ + 3 : NZ + 3 + NZ]
    scratch = refs[NZ + 3 + NZ]
    earlier = [jnp.zeros((PAIR, STATE), F32) for _ in range(2)]
    for k in range(1, NX):
        source = (x - k) & (NX - 1)
        two = between(x_table, x, jnp.minimum(source + 1, x))
        for b in range(2):
            keep = (source < x) & (((source ^ x) > 1) == (b == 1))
            earlier[b] += scaled_pair(only_if(keep, two), others[k - 1][...])
    for slot in range(NZ):
        target = (z + slot) & (NZ - 1)
        for b in range(3):
            scratch[b] = jnp.zeros((PAIR, STATE), F32)
        for back in range(NZ):
            source = (z - back) & (NZ - 1)
            two = only_if(source < target, between(table, target, jnp.minimum(source + 1, target)))
            mixed = source ^ target
            at = (mixed > 1).astype(jnp.int32) + (mixed > 3).astype(jnp.int32)
            scratch[at] = scratch[at] + scaled_pair(two, pieces[back][...])
        for b in range(3):
            outs[slot][b] = scratch[b].astype(BF16)
        start = between(table, target, 0)
        for b in range(2):
            outs[slot][3 + b] = scaled_pair(start, earlier[b]).astype(BF16)


def values_grad_kernel(place, local, write, cum, *refs):
    z = place[1]
    states, out = refs[:NZ], refs[NZ]
    write_rows = write[...]
    for slot in range(NZ):
        pair = (z - slot) & (NZ - 1)
        c = cum[pair]
        rows = dot(states[slot][...], write_rows, NT) * spread(jnp.exp(c[:, TOK - 1 :] - c))
        rows += rows_at(local, pair)
        out[:, pl.ds(pl.multiple_of(pair * PAIR, PAIR), PAIR)] = rows.T.astype(BF16)


def layer_out_kernel(place, local, read, cum, gain, *refs):
    z = place[1]
    buckets, out = refs[:NZ], refs[NZ]
    read_rows = read[...]
    for slot in range(NZ):
        pair = (z - slot) & (NZ - 1)
        decay = jnp.exp(cum[pair])
        rows = rows_at(local, pair)
        for b in range(5):
            rows += dot(buckets[slot][b], read_rows, NT) * spread(gain[LOCAL + b, pair] * decay)
        out[:, pl.ds(pl.multiple_of(pair * PAIR, PAIR), PAIR)] = rows.T.astype(BF16)


def shift(value, axis, apart):
    size = lax.axis_size(axis)
    return lax.ppermute(value, axis, [(i, (i + apart) % size) for i in range(size)])


def deal(pieces):
    return [pieces[0]] + [shift(pieces[d], "seq_1", d) for d in range(1, NZ)]


def around_x(value):
    return [shift(value, "seq_0", k) for k in range(1, NX)]


def ring_scatter(chunk, axis):
    size = lax.axis_size(axis)
    place = lax.axis_index(axis)
    half = size // 2
    ahead, back = chunk((place + half) % size), chunk((place - half + 1) % size)
    for step in range(half - 1, -1, -1):
        ahead = shift(ahead, axis, 1)
        if step > 0:
            ahead = ahead + chunk((place + step) % size)
        if step < half - 1:
            back = shift(back, axis, -1)
            if step > 0:
                back = back + chunk((place - step) % size)
    total = chunk(place).astype(F32) + ahead.astype(F32) + back.astype(F32)
    return total.astype(BF16)


def per_device(tokens, in_weight, write_proj, read_proj, log_decay, level_gain, out_grad):
    x, z = lax.axis_index("seq_0"), lax.axis_index("seq_1")
    place = jnp.stack([x, z]).astype(jnp.int32)
    both = lax.all_gather(
        jnp.concatenate([write_proj, read_proj], axis=1), "head", axis=0, tiled=True
    )
    write, read = both[:, :STATE], both[:, STATE:]
    full_tokens = lax.all_gather(tokens, "head", axis=0, tiled=True)
    weight = lax.all_gather(in_weight, SEQ, axis=0, tiled=True)
    cum = jnp.cumsum(log_decay, axis=1).reshape(NZ, 2, TOK)
    gain = level_gain.reshape(LOCAL + 5, NZ, 2, TOK)

    piece5, piece = shaped((5, PAIR, STATE), BF16), shaped((PAIR, STATE), BF16)
    with_totals = lambda levels: shaped((levels * PAIR + 16, STATE), BF16)
    table_shape = lambda count: shaped((2, count, STATE), F32)
    rows = shaped((NZ * PAIR, TOK), F32)
    natural = shaped((TOK, NZ * PAIR), BF16)

    def local(source, forward, name):
        kernel = lambda *refs: local_kernel(forward, *refs)
        return call(kernel, name, [rows], 0, 5, [pltpu.VMEM((TOK, TOK), F32)])(
            source, read, write, cum, gain
        )[0]

    sent = call(level_grad_kernel, "level_grad", [with_totals(5)] * NZ, 1, 4)(
        place, out_grad, read, cum, gain
    )
    got = deal(sent)
    later, table = call(
        later_sum_kernel,
        "later_sum",
        [with_totals(2), table_shape(16)],
        1,
        NZ,
        [pltpu.VMEM((2, NZ, STATE), F32)],
    )(place, *got)
    *grads, x_table = call(
        state_grad_kernel,
        "state_grad",
        [piece] * NZ + [table_shape(8)],
        1,
        1 + NZ + 3,
        [pltpu.VMEM((2, NZ, STATE), F32)],
    )(place, table, *got, *around_x(later))
    local_grad = local(out_grad, False, "local_bwd")
    values_grad = call(values_grad_kernel, "values_grad", [natural], 1, 3 + NZ)(
        place, local_grad, write, cum, *deal(grads)
    )[0]
    held_tokens, weight = lax.optimization_barrier((full_tokens, weight))
    partial = lax.dot_general(
        held_tokens, values_grad, (((0,), (0,)), ((), ())), preferred_element_type=F32
    ).astype(BF16)
    weight_grad = lax.psum_scatter(partial, "seq_0", scatter_dimension=0, tiled=True)

    values = jnp.dot(full_tokens, weight, preferred_element_type=F32).astype(BF16)
    states = call(state_kernel, "seg_state", [piece] * NZ, 1, 3)(place, values, write, cum)
    got = deal(states)
    block = call(block_sum_kernel, "block_sum", [piece], 1, 1 + NZ)(place, table, *got)[0]
    buckets = call(
        bucket_kernel, "bucket", [piece5] * NZ, 1, 2 + NZ + 3, [pltpu.VMEM((3, PAIR, STATE), F32)]
    )(place, table, x_table, *got, *around_x(block))
    local_out = local(values, True, "local_fwd")
    layer_out = call(layer_out_kernel, "layer_out", [natural], 1, 4 + NZ)(
        place, local_out, read, cum, gain, *deal(buckets)
    )[0]
    weight_grad, layer_out = lax.optimization_barrier((weight_grad, layer_out))
    part = STATE
    weight_grad = ring_scatter(
        lambda at: lax.dynamic_slice_in_dim(weight_grad, at * part, part, axis=0), "seq_1"
    )
    return (layer_out, weight_grad)


def solution(mesh):
    split = Mesh(mesh.devices.reshape(NX, NZ, mesh.shape["head"]), ("seq_0", "seq_1", "head"))
    in_specs = (
        P(SEQ_HEAD, None),
        P(SEQ, "head"),
        P(SEQ_HEAD, None),
        P(SEQ_HEAD, None),
        P("head", SEQ),
        P(None, "head", SEQ),
        P(SEQ, "head"),
    )
    out_specs = (P(SEQ, "head"), P(SEQ, "head"))
    return jax.shard_map(
        per_device, mesh=split, in_specs=in_specs, out_specs=out_specs, check_vma=False
    )
```

```python
import jax
import jax.numpy as jnp
from jax import lax
from jax.experimental import pallas as pl
from jax.experimental.pallas import tpu as pltpu
from jax.sharding import Mesh
from jax.sharding import PartitionSpec as P

HEAD_DIM = 64
STATE = 128
TOK = 512
CH = 64
NZ = 8
NX = 4
PAIR = 2 * HEAD_DIM
LOCAL = 4
SEQ = ("seq_0", "seq_1")
SEQ_HEAD = ("seq_0", "seq_1", "head")
F32 = jnp.float32
BF16 = jnp.bfloat16

NT = (((1,), (1,)), ((), ()))
NN = (((1,), (0,)), ((), ()))


def dot(a, b, dims=NN):
    return lax.dot_general(a, b, dims, preferred_element_type=F32)


def spread(rows, each=HEAD_DIM):
    n, t = rows.shape
    return jnp.concatenate([jnp.broadcast_to(rows[i : i + 1], (each, t)) for i in range(n)], axis=0)


def owner_of(slot_base, slot):
    return (slot_base + slot) & (NZ - 1)


def columns(ref, pair):
    return ref[:, pl.ds(pl.multiple_of(pair * PAIR, PAIR), PAIR)]


def rows_at(ref, pair):
    return ref[pl.ds(pl.multiple_of(pair * PAIR, PAIR), PAIR), :]


def vmem():
    return pl.BlockSpec(memory_space=pltpu.VMEM)


def smem():
    return pl.BlockSpec(memory_space=pltpu.SMEM)


def call(kernel, name, outs, n_smem, n_vmem, scratch=(), flops=0):
    return pl.pallas_call(
        kernel,
        name=name,
        out_shape=outs,
        in_specs=[smem()] * n_smem + [vmem()] * n_vmem,
        out_specs=[vmem() for _ in outs],
        scratch_shapes=scratch,
        compiler_params=pltpu.CompilerParams(vmem_limit_bytes=48 << 20),
    )


def shaped(shape, dtype):
    return jax.ShapeDtypeStruct(shape, dtype)


def split_totals(totals):
    wide = jnp.broadcast_to(totals, (2, STATE))
    high = wide.astype(BF16).astype(F32)
    rest = wide - high
    middle = rest.astype(BF16).astype(F32)
    rows = [high, middle, rest - middle, jnp.zeros((10, STATE), F32)]
    return jnp.concatenate(rows, axis=0).astype(BF16)


def joined_totals(rows):
    rows = rows.astype(F32)
    return rows[0:2] + rows[2:4] + rows[4:6]


def level_grad_kernel(place, grad, read, cum, gain, *outs):
    z = place[1]
    read_rows = read[...]
    for slot in range(NZ):
        pair = owner_of(z, slot)
        rows = columns(grad, pair).astype(F32).T
        c = cum[pair]
        decay = jnp.exp(c)
        for b in range(5):
            scaled = (rows * spread(gain[LOCAL + b, pair] * decay)).astype(BF16)
            outs[slot][b * PAIR : (b + 1) * PAIR, :] = dot(scaled, read_rows).astype(BF16)
        outs[slot][5 * PAIR :, :] = split_totals(c[:, TOK - 1 :])


def state_kernel(place, values, write, cum, *outs):
    z = place[1]
    write_rows = write[...]
    for slot in range(NZ):
        pair = owner_of(z, slot)
        rows = columns(values, pair).astype(F32).T
        c = cum[pair]
        scaled = (rows * spread(jnp.exp(c[:, TOK - 1 :] - c))).astype(BF16)
        outs[slot][...] = dot(scaled, write_rows).astype(BF16)


def local_kernel(forward, source, read, write, cum, gain, out, score_ref):
    score_ref[...] = dot(write[...], read[...], NT)
    half = score_ref[...].astype(BF16)
    row_id = lax.broadcasted_iota(jnp.int32, (128, 128), 0)
    col_id = lax.broadcasted_iota(jnp.int32, (128, 128), 1)
    causal = row_id <= col_id
    crosses = (row_id < CH) & (col_id >= CH)

    def one_pair(pair, carry):
        rows = columns(source, pair).T
        rows_f = rows.astype(F32)
        c = cum[pair]
        c_col = jnp.concatenate([c, jnp.zeros((6, TOK), F32)], axis=0).T
        g0, g1, g2, g3 = (gain[level, pair] for level in range(LOCAL))

        def far(lo, mid, hi, g):
            edge = c[:, mid - 1 : mid]
            before = spread(jnp.exp(edge - c[:, lo:mid]))
            after = spread(g[:, mid:hi] * jnp.exp(c[:, mid:hi] - edge))
            block = half[lo:mid, mid:hi]
            if forward:
                return dot((rows_f[:, lo:mid] * before).astype(BF16), block) * after
            return dot((rows_f[:, mid:hi] * after).astype(BF16), block, NT) * before

        near = []
        for i in range(4):
            lo, hi = i * 128, i * 128 + 128
            score = score_ref[lo:hi, lo:hi]
            parts = []
            for h in range(2):
                differ = c[h : h + 1, lo:hi] - c_col[lo:hi, h : h + 1]
                decays = jnp.exp(jnp.where(causal, differ, -1e30))
                gains = jnp.where(crosses, g1[h : h + 1, lo:hi], g0[h : h + 1, lo:hi])
                weights = (gains * decays * score).astype(BF16)
                parts.append(
                    dot(rows[h * HEAD_DIM : (h + 1) * HEAD_DIM, lo:hi], weights, NN if forward else NT)
                )
            near.append(jnp.concatenate(parts, axis=0))
        wide = far(0, 256, 512, g3)
        left, right = far(0, 128, 256, g2), far(256, 384, 512, g2)
        if forward:
            near[1] += left
            near[3] += right
            near[2] += wide[:, :128]
            near[3] += wide[:, 128:]
        else:
            near[0] += left
            near[2] += right
            near[0] += wide[:, :128]
            near[1] += wide[:, 128:]
        at = pl.ds(pl.multiple_of(pair * PAIR, PAIR), PAIR)
        for i in range(4):
            out[at, i * 128 : i * 128 + 128] = near[i]
        return carry

    lax.fori_loop(0, NZ, one_pair, 0)


def between(table, upper, lower):
    return [
        jnp.exp(table[h, pl.ds(upper, 1), :] - table[h, pl.ds(lower, 1), :]) for h in range(2)
    ]


def only_if(condition, two):
    return [jnp.where(condition, one, 0.0) for one in two]


def scaled_pair(two, value):
    value = value.astype(F32)
    return jnp.concatenate([value[:HEAD_DIM] * two[0], value[HEAD_DIM:] * two[1]], axis=0)


def running_sums(table, count, scratch):
    for h in range(2):
        total = jnp.zeros((1, STATE), F32)
        for i in range(count):
            table[h, i : i + 1, :] = total
            total = total + scratch[h, i : i + 1, :]
        table[h, count : count + 1, :] = total


def later_sum_kernel(place, *refs):
    z = place[1]
    pieces, out, table, scratch = refs[:NZ], refs[NZ], refs[NZ + 1], refs[NZ + 2]
    for slot in range(NZ):
        source = (z - slot) & (NZ - 1)
        totals = joined_totals(pieces[slot][5 * PAIR :, :])
        for h in range(2):
            scratch[h, pl.ds(source, 1), :] = totals[h : h + 1]
    running_sums(table, NZ, scratch)
    starts = [between(table, (z - slot) & (NZ - 1), 0) for slot in range(NZ)]
    for b in range(2):
        total = jnp.zeros((PAIR, STATE), F32)
        for slot in range(NZ):
            total += scaled_pair(starts[slot], pieces[slot][(3 + b) * PAIR : (4 + b) * PAIR, :])
        out[b * PAIR : (b + 1) * PAIR, :] = total.astype(BF16)
    whole = jnp.concatenate([table[h, NZ : NZ + 1, :1] for h in range(2)], axis=0)
    out[2 * PAIR :, :] = split_totals(whole)


def state_grad_kernel(place, table, *refs):
    x, z = place[0], place[1]
    pieces, others, outs = refs[:NZ], refs[NZ : NZ + 3], refs[NZ + 3 : NZ + 3 + NZ]
    x_table, scratch = refs[NZ + 3 + NZ :]
    for h in range(2):
        scratch[h, pl.ds(x, 1), :] = table[h, NZ : NZ + 1, :]
    for k in range(1, NX):
        source = (x - k) & (NX - 1)
        totals = joined_totals(others[k - 1][2 * PAIR :, :])
        for h in range(2):
            scratch[h, pl.ds(source, 1), :] = totals[h : h + 1]
    running_sums(x_table, NX, scratch)
    later = jnp.zeros((PAIR, STATE), F32)
    for k in range(1, NX):
        source = (x - k) & (NX - 1)
        two = only_if(source > x, between(x_table, source, jnp.minimum(x + 1, source)))
        level = ((source ^ x) > 1).astype(jnp.int32)
        later += scaled_pair(two, rows_at(others[k - 1], level))
    for slot in range(NZ):
        target = (z + slot) & (NZ - 1)
        total = scaled_pair(between(table, NZ, target + 1), later)
        for back in range(NZ):
            source = (z - back) & (NZ - 1)
            two = only_if(source > target, between(table, source, jnp.minimum(target + 1, source)))
            mixed = source ^ target
            level = (mixed > 1).astype(jnp.int32) + (mixed > 3).astype(jnp.int32)
            total += scaled_pair(two, rows_at(pieces[back], level))
        outs[slot][...] = total.astype(BF16)


def block_sum_kernel(place, table, *refs):
    z = place[1]
    pieces, out = refs[:NZ], refs[NZ]
    total = jnp.zeros((PAIR, STATE), F32)
    for slot in range(NZ):
        source = (z - slot) & (NZ - 1)
        total += scaled_pair(between(table, NZ, source + 1), pieces[slot][...])
    out[...] = total.astype(BF16)


def bucket_kernel(place, table, x_table, *refs):
    x, z = place[0], place[1]
    pieces, others, outs = refs[:NZ], refs[NZ : NZ + 3], refs[NZ + 3 : NZ + 3 + NZ]
    scratch = refs[NZ + 3 + NZ]
    earlier = [jnp.zeros((PAIR, STATE), F32) for _ in range(2)]
    for k in range(1, NX):
        source = (x - k) & (NX - 1)
        two = between(x_table, x, jnp.minimum(source + 1, x))
        for b in range(2):
            keep = (source < x) & (((source ^ x) > 1) == (b == 1))
            earlier[b] += scaled_pair(only_if(keep, two), others[k - 1][...])
    for slot in range(NZ):
        target = (z + slot) & (NZ - 1)
        for b in range(3):
            scratch[b] = jnp.zeros((PAIR, STATE), F32)
        for back in range(NZ):
            source = (z - back) & (NZ - 1)
            two = only_if(source < target, between(table, target, jnp.minimum(source + 1, target)))
            mixed = source ^ target
            at = (mixed > 1).astype(jnp.int32) + (mixed > 3).astype(jnp.int32)
            scratch[at] = scratch[at] + scaled_pair(two, pieces[back][...])
        for b in range(3):
            outs[slot][b] = scratch[b].astype(BF16)
        start = between(table, target, 0)
        for b in range(2):
            outs[slot][3 + b] = scaled_pair(start, earlier[b]).astype(BF16)


def values_grad_kernel(place, local, write, cum, *refs):
    z = place[1]
    states, out = refs[:NZ], refs[NZ]
    write_rows = write[...]
    for slot in range(NZ):
        pair = (z - slot) & (NZ - 1)
        c = cum[pair]
        rows = dot(states[slot][...], write_rows, NT) * spread(jnp.exp(c[:, TOK - 1 :] - c))
        rows += rows_at(local, pair)
        out[:, pl.ds(pl.multiple_of(pair * PAIR, PAIR), PAIR)] = rows.T.astype(BF16)


def layer_out_kernel(place, local, read, cum, gain, *refs):
    z = place[1]
    buckets, out = refs[:NZ], refs[NZ]
    read_rows = read[...]
    for slot in range(NZ):
        pair = (z - slot) & (NZ - 1)
        decay = jnp.exp(cum[pair])
        rows = rows_at(local, pair)
        for b in range(5):
            rows += dot(buckets[slot][b], read_rows, NT) * spread(gain[LOCAL + b, pair] * decay)
        out[:, pl.ds(pl.multiple_of(pair * PAIR, PAIR), PAIR)] = rows.T.astype(BF16)


def shift(value, axis, apart):
    size = lax.axis_size(axis)
    return lax.ppermute(value, axis, [(i, (i + apart) % size) for i in range(size)])


def deal(pieces):
    return [pieces[0]] + [shift(pieces[d], "seq_1", d) for d in range(1, NZ)]


def around_x(value):
    return [shift(value, "seq_0", k) for k in range(1, NX)]


def swapped_cores(value):
    return lax.ppermute(value, "head", [(i, i ^ 1) for i in range(8)])


def gather_tokens(tokens, also):
    head = lax.axis_index("head")
    y, core = head // 2, head % 2
    half = tokens.shape[0] // 2
    up, down = shift(tokens, "head", 2), shift(tokens, "head", -2)
    up, down, also = lax.optimization_barrier((up, down, also))
    far = [shift(up[:half], "head", 2), shift(down[half:], "head", -2)]
    mine = jnp.zeros((4,) + tokens.shape, tokens.dtype)
    at = lambda k: ((y - k) & 3, 0, 0)
    mine = lax.dynamic_update_slice(mine, tokens[None], at(0))
    mine = lax.dynamic_update_slice(mine, up[None], at(1))
    mine = lax.dynamic_update_slice(mine, jnp.concatenate(far, axis=0)[None], at(2))
    mine = lax.dynamic_update_slice(mine, down[None], at(3))
    other = swapped_cores(mine)
    first = jnp.where(core == 0, mine, other)
    second = jnp.where(core == 0, other, mine)
    return jnp.stack([first, second], axis=1).reshape(-1, tokens.shape[1]), far, also


def scatter_over_x(tokens, grads, x, states, forward):
    width = tokens.shape[1] // NX
    half = grads.shape[1] // 2

    def chunk(block, columns=slice(None)):
        rows = lax.dynamic_slice_in_dim(tokens, (block & (NX - 1)) * width, width, axis=1)
        return lax.dot_general(
            rows, grads[:, columns], (((0,), (0,)), ((), ())), preferred_element_type=F32
        )

    far = chunk(x + 2).astype(BF16)
    ahead, back = shift(far[:, :half], "seq_0", 1), shift(far[:, half:], "seq_0", -1)
    to_ahead, to_back = chunk(x + 1), chunk(x - 1)
    ahead, back, states = lax.optimization_barrier((ahead, back, states))
    to_ahead = jnp.concatenate([to_ahead[:, :half] + ahead.astype(F32), to_ahead[:, half:]], axis=1)
    to_back = jnp.concatenate([to_back[:, :half], to_back[:, half:] + back.astype(F32)], axis=1)
    ahead = shift(to_ahead.astype(BF16), "seq_0", 1)
    back = shift(to_back.astype(BF16), "seq_0", -1)
    buckets = forward(states)
    ahead, back, buckets = lax.optimization_barrier((ahead, back, buckets))
    return (chunk(x) + ahead.astype(F32) + back.astype(F32)).astype(BF16), buckets


def ring_scatter(chunk, axis):
    size = lax.axis_size(axis)
    place = lax.axis_index(axis)
    half = size // 2
    ahead, back = chunk((place + half) % size), chunk((place - half + 1) % size)
    for step in range(half - 1, -1, -1):
        ahead = shift(ahead, axis, 1)
        if step > 0:
            ahead = ahead + chunk((place + step) % size)
        if step < half - 1:
            back = shift(back, axis, -1)
            if step > 0:
                back = back + chunk((place - step) % size)
    total = chunk(place).astype(F32) + ahead.astype(F32) + back.astype(F32)
    return total.astype(BF16)


def per_device(tokens, in_weight, write_proj, read_proj, log_decay, level_gain, out_grad):
    x, z = lax.axis_index("seq_0"), lax.axis_index("seq_1")
    place = jnp.stack([x, z]).astype(jnp.int32)
    both = lax.all_gather(
        jnp.concatenate([write_proj, read_proj], axis=1), "head", axis=0, tiled=True
    )
    write, read = both[:, :STATE], both[:, STATE:]
    full_tokens, far, read = gather_tokens(tokens, read)
    weight = lax.all_gather(in_weight, SEQ, axis=0, tiled=True)
    cum = jnp.cumsum(log_decay, axis=1).reshape(NZ, 2, TOK)
    gain = level_gain.reshape(LOCAL + 5, NZ, 2, TOK)

    piece5, piece = shaped((5, PAIR, STATE), BF16), shaped((PAIR, STATE), BF16)
    with_totals = lambda levels: shaped((levels * PAIR + 16, STATE), BF16)
    table_shape = lambda count: shaped((2, count, STATE), F32)
    rows = shaped((NZ * PAIR, TOK), F32)
    natural = shaped((TOK, NZ * PAIR), BF16)

    def local(source, forward, name):
        kernel = lambda *refs: local_kernel(forward, *refs)
        return call(kernel, name, [rows], 0, 5, [pltpu.VMEM((TOK, TOK), F32)])(
            source, read, write, cum, gain
        )[0]

    sent = call(level_grad_kernel, "level_grad", [with_totals(5)] * NZ, 1, 4)(
        place, out_grad, read, cum, gain
    )
    sent, _ = lax.optimization_barrier((sent, far))
    got = deal(sent)
    later, table = call(
        later_sum_kernel,
        "later_sum",
        [with_totals(2), table_shape(16)],
        1,
        NZ,
        [pltpu.VMEM((2, NZ, STATE), F32)],
    )(place, *got)
    *grads, x_table = call(
        state_grad_kernel,
        "state_grad",
        [piece] * NZ + [table_shape(8)],
        1,
        1 + NZ + 3,
        [pltpu.VMEM((2, NZ, STATE), F32)],
    )(place, table, *got, *around_x(later))
    local_grad = local(out_grad, False, "local_bwd")
    values_grad = call(values_grad_kernel, "values_grad", [natural], 1, 3 + NZ)(
        place, local_grad, write, cum, *deal(grads)
    )[0]
    values = jnp.dot(full_tokens, weight, preferred_element_type=F32).astype(BF16)
    states = call(state_kernel, "seg_state", [piece] * NZ, 1, 3)(place, values, write, cum)

    def combined(states):
        got = deal(states)
        block = call(block_sum_kernel, "block_sum", [piece], 1, 1 + NZ)(place, table, *got)[0]
        sent = call(
            bucket_kernel,
            "bucket",
            [piece5] * NZ,
            1,
            2 + NZ + 3,
            [pltpu.VMEM((3, PAIR, STATE), F32)],
        )(place, table, x_table, *got, *around_x(block))
        return deal(sent)

    weight_grad, buckets = scatter_over_x(full_tokens, values_grad, x, states, combined)
    local_out = local(values, True, "local_fwd")
    layer_out = call(layer_out_kernel, "layer_out", [natural], 1, 4 + NZ)(
        place, local_out, read, cum, gain, *buckets
    )[0]
    part = STATE
    weight_grad = ring_scatter(
        lambda at: lax.dynamic_slice_in_dim(weight_grad, at * part, part, axis=0), "seq_1"
    )
    return (layer_out, weight_grad)


def solution(mesh):
    split = Mesh(mesh.devices.reshape(NX, NZ, mesh.shape["head"]), ("seq_0", "seq_1", "head"))
    in_specs = (
        P(SEQ_HEAD, None),
        P(SEQ, "head"),
        P(SEQ_HEAD, None),
        P(SEQ_HEAD, None),
        P("head", SEQ),
        P(None, "head", SEQ),
        P(SEQ, "head"),
    )
    out_specs = (P(SEQ, "head"), P(SEQ, "head"))
    return jax.shard_map(
        per_device, mesh=split, in_specs=in_specs, out_specs=out_specs, check_vma=False
    )
```

```python
import jax
import jax.numpy as jnp
from jax import lax
from jax.experimental import pallas as pl
from jax.experimental.pallas import tpu as pltpu
from jax.sharding import Mesh
from jax.sharding import PartitionSpec as P

HEAD_DIM = 64
STATE = 128
TOK = 512
CH = 64
NZ = 8
NX = 4
PAIR = 2 * HEAD_DIM
LOCAL = 4
SEQ = ("seq_0", "seq_1")
SEQ_HEAD = ("seq_0", "seq_1", "head")
F32 = jnp.float32
BF16 = jnp.bfloat16

NT = (((1,), (1,)), ((), ()))
NN = (((1,), (0,)), ((), ()))


def dot(a, b, dims=NN):
    return lax.dot_general(a, b, dims, preferred_element_type=F32)


def spread(rows, each=HEAD_DIM):
    n, t = rows.shape
    return jnp.concatenate([jnp.broadcast_to(rows[i : i + 1], (each, t)) for i in range(n)], axis=0)


def owner_of(slot_base, slot):
    return (slot_base + slot) & (NZ - 1)


def columns(ref, pair):
    return ref[:, pl.ds(pl.multiple_of(pair * PAIR, PAIR), PAIR)]


def row_block(index):
    return pl.ds(pl.multiple_of(index * PAIR, PAIR), PAIR)


def rows_at(ref, index):
    return ref[row_block(index), :]


def vmem():
    return pl.BlockSpec(memory_space=pltpu.VMEM)


def smem():
    return pl.BlockSpec(memory_space=pltpu.SMEM)


def call(kernel, name, outs, n_smem, n_vmem, scratch=(), flops=0):
    return pl.pallas_call(
        kernel,
        name=name,
        out_shape=outs,
        in_specs=[smem()] * n_smem + [vmem()] * n_vmem,
        out_specs=[vmem() for _ in outs],
        scratch_shapes=scratch,
        compiler_params=pltpu.CompilerParams(vmem_limit_bytes=48 << 20),
    )


def shaped(shape, dtype):
    return jax.ShapeDtypeStruct(shape, dtype)


def split_totals(totals):
    wide = jnp.broadcast_to(totals, (2, STATE))
    high = wide.astype(BF16).astype(F32)
    rest = wide - high
    middle = rest.astype(BF16).astype(F32)
    rows = [high, middle, rest - middle, jnp.zeros((10, STATE), F32)]
    return jnp.concatenate(rows, axis=0).astype(BF16)


def joined_totals(rows):
    rows = rows.astype(F32)
    return rows[0:2] + rows[2:4] + rows[4:6]


def level_grad_kernel(place, grad, read, cum, gain, *outs):
    z = place[1]
    read_rows = read[...]
    for slot in range(NZ):
        pair = owner_of(z, slot)
        rows = columns(grad, pair).astype(F32).T
        c = cum[pair]
        decay = jnp.exp(c)

        def one_level(b, carry, slot=slot, pair=pair, rows=rows, decay=decay):
            scaled = (rows * spread(gain[LOCAL + b, pair] * decay)).astype(BF16)
            outs[slot][row_block(b), :] = dot(scaled, read_rows).astype(BF16)
            return carry

        lax.fori_loop(0, 5, one_level, 0)
        outs[slot][5 * PAIR :, :] = split_totals(c[:, TOK - 1 :])


def state_kernel(place, values, write, cum, *outs):
    z = place[1]
    write_rows = write[...]
    for slot in range(NZ):
        pair = owner_of(z, slot)
        rows = columns(values, pair).astype(F32).T
        c = cum[pair]
        scaled = (rows * spread(jnp.exp(c[:, TOK - 1 :] - c))).astype(BF16)
        outs[slot][...] = dot(scaled, write_rows).astype(BF16)


def local_kernel(forward, source, read, write, cum, gain, out, score_ref):
    score_ref[...] = dot(write[...], read[...], NT)
    half = score_ref[...].astype(BF16)
    row_id = lax.broadcasted_iota(jnp.int32, (128, 128), 0)
    col_id = lax.broadcasted_iota(jnp.int32, (128, 128), 1)
    causal = row_id <= col_id
    crosses = (row_id < CH) & (col_id >= CH)

    def one_pair(pair, carry):
        rows = columns(source, pair).T
        rows_f = rows.astype(F32)
        c = cum[pair]
        c_col = jnp.concatenate([c, jnp.zeros((6, TOK), F32)], axis=0).T
        g0, g1, g2, g3 = (gain[level, pair] for level in range(LOCAL))

        def far(lo, mid, hi, g):
            edge = c[:, mid - 1 : mid]
            before = spread(jnp.exp(edge - c[:, lo:mid]))
            after = spread(g[:, mid:hi] * jnp.exp(c[:, mid:hi] - edge))
            block = half[lo:mid, mid:hi]
            if forward:
                return dot((rows_f[:, lo:mid] * before).astype(BF16), block) * after
            return dot((rows_f[:, mid:hi] * after).astype(BF16), block, NT) * before

        near = []
        for i in range(4):
            lo, hi = i * 128, i * 128 + 128
            score = score_ref[lo:hi, lo:hi]
            parts = []
            for h in range(2):
                differ = c[h : h + 1, lo:hi] - c_col[lo:hi, h : h + 1]
                decays = jnp.exp(jnp.where(causal, differ, -1e30))
                gains = jnp.where(crosses, g1[h : h + 1, lo:hi], g0[h : h + 1, lo:hi])
                weights = (gains * decays * score).astype(BF16)
                parts.append(
                    dot(rows[h * HEAD_DIM : (h + 1) * HEAD_DIM, lo:hi], weights, NN if forward else NT)
                )
            near.append(jnp.concatenate(parts, axis=0))
        wide = far(0, 256, 512, g3)
        left, right = far(0, 128, 256, g2), far(256, 384, 512, g2)
        if forward:
            near[1] += left
            near[3] += right
            near[2] += wide[:, :128]
            near[3] += wide[:, 128:]
        else:
            near[0] += left
            near[2] += right
            near[0] += wide[:, :128]
            near[1] += wide[:, 128:]
        at = pl.ds(pl.multiple_of(pair * PAIR, PAIR), PAIR)
        for i in range(4):
            out[at, i * 128 : i * 128 + 128] = near[i]
        return carry

    lax.fori_loop(0, NZ, one_pair, 0)


def between(table, upper, lower):
    return [
        jnp.exp(table[h, pl.ds(upper, 1), :] - table[h, pl.ds(lower, 1), :]) for h in range(2)
    ]


def only_if(condition, two):
    return [jnp.where(condition, one, 0.0) for one in two]


def scaled_pair(two, value):
    value = value.astype(F32)
    return jnp.concatenate([value[:HEAD_DIM] * two[0], value[HEAD_DIM:] * two[1]], axis=0)


def running_sums(table, count, scratch):
    for h in range(2):
        total = jnp.zeros((1, STATE), F32)
        for i in range(count):
            table[h, i : i + 1, :] = total
            total = total + scratch[h, i : i + 1, :]
        table[h, count : count + 1, :] = total


def later_sum_kernel(place, *refs):
    z = place[1]
    pieces, out, table, scratch = refs[:NZ], refs[NZ], refs[NZ + 1], refs[NZ + 2]
    for slot in range(NZ):
        source = (z - slot) & (NZ - 1)
        totals = joined_totals(pieces[slot][5 * PAIR :, :])
        for h in range(2):
            scratch[h, pl.ds(source, 1), :] = totals[h : h + 1]
    running_sums(table, NZ, scratch)
    starts = [between(table, (z - slot) & (NZ - 1), 0) for slot in range(NZ)]
    for b in range(2):
        total = jnp.zeros((PAIR, STATE), F32)
        for slot in range(NZ):
            total += scaled_pair(starts[slot], pieces[slot][(3 + b) * PAIR : (4 + b) * PAIR, :])
        out[b * PAIR : (b + 1) * PAIR, :] = total.astype(BF16)
    whole = jnp.concatenate([table[h, NZ : NZ + 1, :1] for h in range(2)], axis=0)
    out[2 * PAIR :, :] = split_totals(whole)


def state_grad_kernel(place, table, *refs):
    x, z = place[0], place[1]
    pieces, others, outs = refs[:NZ], refs[NZ : NZ + 3], refs[NZ + 3 : NZ + 3 + NZ]
    x_table, scratch, ordered = refs[NZ + 3 + NZ :]
    for back in range(NZ):
        ordered[(z - back) & (NZ - 1)] = pieces[back][: 3 * PAIR, :]
    for h in range(2):
        scratch[h, pl.ds(x, 1), :] = table[h, NZ : NZ + 1, :]
    for k in range(1, NX):
        source = (x - k) & (NX - 1)
        totals = joined_totals(others[k - 1][2 * PAIR :, :])
        for h in range(2):
            scratch[h, pl.ds(source, 1), :] = totals[h : h + 1]
    running_sums(x_table, NX, scratch)
    later = jnp.zeros((PAIR, STATE), F32)
    for k in range(1, NX):
        source = (x - k) & (NX - 1)
        two = only_if(source > x, between(x_table, source, jnp.minimum(x + 1, source)))
        level = ((source ^ x) > 1).astype(jnp.int32)
        later += scaled_pair(two, rows_at(others[k - 1], level))
    for slot in range(NZ):
        target = (z + slot) & (NZ - 1)

        def add_source(source, total, target=target):
            two = only_if(source > target, between(table, source, jnp.minimum(target + 1, source)))
            mixed = source ^ target
            level = (mixed > 1).astype(jnp.int32) + (mixed > 3).astype(jnp.int32)
            return total + scaled_pair(two, ordered[source, row_block(level), :])

        first = scaled_pair(between(table, NZ, target + 1), later)
        outs[slot][...] = lax.fori_loop(0, NZ, add_source, first).astype(BF16)


def block_sum_kernel(place, table, *refs):
    z = place[1]
    pieces, out = refs[:NZ], refs[NZ]
    total = jnp.zeros((PAIR, STATE), F32)
    for slot in range(NZ):
        source = (z - slot) & (NZ - 1)
        total += scaled_pair(between(table, NZ, source + 1), pieces[slot][...])
    out[...] = total.astype(BF16)


def bucket_kernel(place, table, x_table, *refs):
    x, z = place[0], place[1]
    pieces, others, outs = refs[:NZ], refs[NZ : NZ + 3], refs[NZ + 3 : NZ + 3 + NZ]
    scratch, ordered = refs[NZ + 3 + NZ :]
    for back in range(NZ):
        ordered[(z - back) & (NZ - 1)] = pieces[back][...]
    earlier = [jnp.zeros((PAIR, STATE), F32) for _ in range(2)]
    for k in range(1, NX):
        source = (x - k) & (NX - 1)
        two = between(x_table, x, jnp.minimum(source + 1, x))
        for b in range(2):
            keep = (source < x) & (((source ^ x) > 1) == (b == 1))
            earlier[b] += scaled_pair(only_if(keep, two), others[k - 1][...])
    for slot in range(NZ):
        target = (z + slot) & (NZ - 1)
        for b in range(3):
            scratch[b] = jnp.zeros((PAIR, STATE), F32)

        def add_source(source, carry, target=target):
            two = only_if(source < target, between(table, target, jnp.minimum(source + 1, target)))
            mixed = source ^ target
            at = (mixed > 1).astype(jnp.int32) + (mixed > 3).astype(jnp.int32)
            scratch[at] = scratch[at] + scaled_pair(two, ordered[source])
            return carry

        lax.fori_loop(0, NZ, add_source, 0)
        for b in range(3):
            outs[slot][b] = scratch[b].astype(BF16)
        start = between(table, target, 0)
        for b in range(2):
            outs[slot][3 + b] = scaled_pair(start, earlier[b]).astype(BF16)


def values_grad_kernel(place, local, write, cum, *refs):
    z = place[1]
    states, out = refs[:NZ], refs[NZ]
    write_rows = write[...]
    for slot in range(NZ):
        pair = (z - slot) & (NZ - 1)
        c = cum[pair]
        rows = dot(states[slot][...], write_rows, NT) * spread(jnp.exp(c[:, TOK - 1 :] - c))
        rows += rows_at(local, pair)
        out[:, pl.ds(pl.multiple_of(pair * PAIR, PAIR), PAIR)] = rows.T.astype(BF16)


def layer_out_kernel(place, local, read, cum, gain, *refs):
    z = place[1]
    buckets, out, total = refs[:NZ], refs[NZ], refs[NZ + 1]
    read_rows = read[...]
    for slot in range(NZ):
        pair = (z - slot) & (NZ - 1)
        decay = jnp.exp(cum[pair])
        total[...] = rows_at(local, pair)

        def one_level(b, carry, slot=slot, pair=pair, decay=decay):
            part = dot(buckets[slot][b], read_rows, NT)
            total[...] += part * spread(gain[LOCAL + b, pair] * decay)
            return carry

        lax.fori_loop(0, 5, one_level, 0)
        out[:, row_block(pair)] = total[...].T.astype(BF16)


def shift(value, axis, apart):
    size = lax.axis_size(axis)
    return lax.ppermute(value, axis, [(i, (i + apart) % size) for i in range(size)])


def deal(pieces):
    return [pieces[0]] + [shift(pieces[d], "seq_1", d) for d in range(1, NZ)]


def around_x(value):
    return [shift(value, "seq_0", k) for k in range(1, NX)]


def ring_scatter(chunk, axis):
    size = lax.axis_size(axis)
    place = lax.axis_index(axis)
    half = size // 2
    ahead, back = chunk((place + half) % size), chunk((place - half + 1) % size)
    for step in range(half - 1, -1, -1):
        ahead = shift(ahead, axis, 1)
        if step > 0:
            ahead = ahead + chunk((place + step) % size)
        if step < half - 1:
            back = shift(back, axis, -1)
            if step > 0:
                back = back + chunk((place - step) % size)
    total = chunk(place).astype(F32) + ahead.astype(F32) + back.astype(F32)
    return total.astype(BF16)


def per_device(tokens, in_weight, write_proj, read_proj, log_decay, level_gain, out_grad):
    x, z = lax.axis_index("seq_0"), lax.axis_index("seq_1")
    place = jnp.stack([x, z]).astype(jnp.int32)
    both = lax.all_gather(
        jnp.concatenate([write_proj, read_proj], axis=1), "head", axis=0, tiled=True
    )
    write, read = both[:, :STATE], both[:, STATE:]
    full_tokens = lax.all_gather(tokens, "head", axis=0, tiled=True)
    weight = lax.all_gather(in_weight, SEQ, axis=0, tiled=True)
    cum = jnp.cumsum(log_decay, axis=1).reshape(NZ, 2, TOK)
    gain = level_gain.reshape(LOCAL + 5, NZ, 2, TOK)

    piece5, piece = shaped((5, PAIR, STATE), BF16), shaped((PAIR, STATE), BF16)
    with_totals = lambda levels: shaped((levels * PAIR + 16, STATE), BF16)
    table_shape = lambda count: shaped((2, count, STATE), F32)
    rows = shaped((NZ * PAIR, TOK), F32)
    natural = shaped((TOK, NZ * PAIR), BF16)

    def local(source, forward, name):
        kernel = lambda *refs: local_kernel(forward, *refs)
        return call(kernel, name, [rows], 0, 5, [pltpu.VMEM((TOK, TOK), F32)])(
            source, read, write, cum, gain
        )[0]

    sent = call(level_grad_kernel, "level_grad", [with_totals(5)] * NZ, 1, 4)(
        place, out_grad, read, cum, gain
    )
    got = deal(sent)
    later, table = call(
        later_sum_kernel,
        "later_sum",
        [with_totals(2), table_shape(16)],
        1,
        NZ,
        [pltpu.VMEM((2, NZ, STATE), F32)],
    )(place, *got)
    *grads, x_table = call(
        state_grad_kernel,
        "state_grad",
        [piece] * NZ + [table_shape(8)],
        1,
        1 + NZ + 3,
        [pltpu.VMEM((2, NZ, STATE), F32), pltpu.VMEM((NZ, 3 * PAIR, STATE), BF16)],
    )(place, table, *got, *around_x(later))
    local_grad = local(out_grad, False, "local_bwd")
    values_grad = call(values_grad_kernel, "values_grad", [natural], 1, 3 + NZ)(
        place, local_grad, write, cum, *deal(grads)
    )[0]
    contract = (((0,), (0,)), ((), ()))
    split = 3 * values_grad.shape[1] // 4
    partial, early = (
        lax.dot_general(full_tokens, part, contract, preferred_element_type=F32).astype(BF16)
        for part in (values_grad[:, :split], values_grad[:, split:])
    )
    early = early.reshape(NX, NZ, STATE, -1)
    early = ring_scatter(
        lambda at: lax.dynamic_index_in_dim(early, at, 1, keepdims=False), "seq_1"
    ).reshape(NX * STATE, -1)
    partial, early, weight = lax.optimization_barrier((partial, early, weight))
    weight_grad = lax.psum_scatter(partial, "seq_0", scatter_dimension=0, tiled=True)

    values = jnp.dot(full_tokens, weight, preferred_element_type=F32).astype(BF16)
    states = call(state_kernel, "seg_state", [piece] * NZ, 1, 3)(place, values, write, cum)
    got = deal(states)
    block = call(block_sum_kernel, "block_sum", [piece], 1, 1 + NZ)(place, table, *got)[0]
    buckets = call(
        bucket_kernel, "bucket", [piece5] * NZ, 1, 2 + NZ + 3,
        [pltpu.VMEM((3, PAIR, STATE), F32), pltpu.VMEM((NZ, PAIR, STATE), BF16)],
    )(place, table, x_table, *got, *around_x(block))
    local_out = local(values, True, "local_fwd")
    layer_out = call(
        layer_out_kernel, "layer_out", [natural], 1, 4 + NZ, [pltpu.VMEM((PAIR, TOK), F32)]
    )(
        place, local_out, read, cum, gain, *deal(buckets)
    )[0]
    weight_grad, layer_out, early = lax.optimization_barrier((weight_grad, layer_out, early))
    early = lax.psum_scatter(early, "seq_0", scatter_dimension=0, tiled=True)
    weight_grad = ring_scatter(
        lambda at: lax.dynamic_slice_in_dim(weight_grad, at * STATE, STATE, axis=0), "seq_1"
    )
    return (layer_out, jnp.concatenate([weight_grad, early], axis=1))


def solution(mesh):
    split = Mesh(mesh.devices.reshape(NX, NZ, mesh.shape["head"]), ("seq_0", "seq_1", "head"))
    in_specs = (
        P(SEQ_HEAD, None),
        P(SEQ, "head"),
        P(SEQ_HEAD, None),
        P(SEQ_HEAD, None),
        P("head", SEQ),
        P(None, "head", SEQ),
        P(SEQ, "head"),
    )
    out_specs = (P(SEQ, "head"), P(SEQ, "head"))
    return jax.shard_map(
        per_device, mesh=split, in_specs=in_specs, out_specs=out_specs, check_vma=False
    )
```

```python
import jax
import jax.numpy as jnp
from jax import lax
from jax.experimental import pallas as pl
from jax.experimental.pallas import tpu as pltpu
from jax.sharding import Mesh
from jax.sharding import PartitionSpec as P

HEAD_DIM = 64
STATE = 128
TOK = 512
CH = 64
NZ = 8
NX = 4
PAIR = 2 * HEAD_DIM
LOCAL = 4
SEQ = ("seq_0", "seq_1")
SEQ_HEAD = ("seq_0", "seq_1", "head")
F32 = jnp.float32
BF16 = jnp.bfloat16

NT = (((1,), (1,)), ((), ()))
NN = (((1,), (0,)), ((), ()))


def dot(a, b, dims=NN):
    return lax.dot_general(a, b, dims, preferred_element_type=F32)


def spread(rows, each=HEAD_DIM):
    n, t = rows.shape
    return jnp.concatenate([jnp.broadcast_to(rows[i : i + 1], (each, t)) for i in range(n)], axis=0)


def owner_of(slot_base, slot):
    return (slot_base + slot) & (NZ - 1)


def columns(ref, pair):
    return ref[:, pl.ds(pl.multiple_of(pair * PAIR, PAIR), PAIR)]


def row_block(index):
    return pl.ds(pl.multiple_of(index * PAIR, PAIR), PAIR)


def rows_at(ref, index):
    return ref[row_block(index), :]


def vmem():
    return pl.BlockSpec(memory_space=pltpu.VMEM)


def smem():
    return pl.BlockSpec(memory_space=pltpu.SMEM)


def call(kernel, name, outs, n_smem, n_vmem, scratch=(), flops=0):
    return pl.pallas_call(
        kernel,
        name=name,
        out_shape=outs,
        in_specs=[smem()] * n_smem + [vmem()] * n_vmem,
        out_specs=[vmem() for _ in outs],
        scratch_shapes=scratch,
        compiler_params=pltpu.CompilerParams(vmem_limit_bytes=48 << 20),
    )


def shaped(shape, dtype):
    return jax.ShapeDtypeStruct(shape, dtype)


def split_totals(totals):
    wide = jnp.broadcast_to(totals, (2, STATE))
    high = wide.astype(BF16).astype(F32)
    rest = wide - high
    middle = rest.astype(BF16).astype(F32)
    rows = [high, middle, rest - middle, jnp.zeros((10, STATE), F32)]
    return jnp.concatenate(rows, axis=0).astype(BF16)


def joined_totals(rows):
    rows = rows.astype(F32)
    return rows[0:2] + rows[2:4] + rows[4:6]


def level_grad_kernel(place, grad, read, cum, gain, out):
    z = place[1]
    outs = sent_by_slot(out, z)
    read_rows = read[...]
    for slot in range(NZ):
        pair = owner_of(z, slot)
        rows = columns(grad, pair).astype(F32).T
        c = cum[pair]
        decay = jnp.exp(c)
        for b in range(5):
            scaled = (rows * spread(gain[LOCAL + b, pair] * decay)).astype(BF16)
            outs[slot][b * PAIR : (b + 1) * PAIR, :] = dot(scaled, read_rows).astype(BF16)
        outs[slot][5 * PAIR :, :] = split_totals(c[:, TOK - 1 :])


def state_kernel(place, values, write, cum, out):
    z = place[1]
    outs = sent_by_slot(out, z)
    write_rows = write[...]
    for slot in range(NZ):
        pair = owner_of(z, slot)
        rows = columns(values, pair).astype(F32).T
        c = cum[pair]
        scaled = (rows * spread(jnp.exp(c[:, TOK - 1 :] - c))).astype(BF16)
        outs[slot][...] = dot(scaled, write_rows).astype(BF16)


def local_kernel(forward, source, read, write, cum, gain, out, score_ref):
    score_ref[...] = dot(write[...], read[...], NT)
    half = score_ref[...].astype(BF16)
    row_id = lax.broadcasted_iota(jnp.int32, (128, 128), 0)
    col_id = lax.broadcasted_iota(jnp.int32, (128, 128), 1)
    causal = row_id <= col_id
    crosses = (row_id < CH) & (col_id >= CH)

    def one_pair(pair, carry):
        rows = columns(source, pair).T
        rows_f = rows.astype(F32)
        c = cum[pair]
        c_col = jnp.concatenate([c, jnp.zeros((6, TOK), F32)], axis=0).T
        g0, g1, g2, g3 = (gain[level, pair] for level in range(LOCAL))

        def far(lo, mid, hi, g):
            edge = c[:, mid - 1 : mid]
            before = spread(jnp.exp(edge - c[:, lo:mid]))
            after = spread(g[:, mid:hi] * jnp.exp(c[:, mid:hi] - edge))
            block = half[lo:mid, mid:hi]
            if forward:
                return dot((rows_f[:, lo:mid] * before).astype(BF16), block) * after
            return dot((rows_f[:, mid:hi] * after).astype(BF16), block, NT) * before

        near = []
        for i in range(4):
            lo, hi = i * 128, i * 128 + 128
            score = score_ref[lo:hi, lo:hi]
            parts = []
            for h in range(2):
                differ = c[h : h + 1, lo:hi] - c_col[lo:hi, h : h + 1]
                decays = jnp.exp(jnp.where(causal, differ, -1e30))
                gains = jnp.where(crosses, g1[h : h + 1, lo:hi], g0[h : h + 1, lo:hi])
                weights = (gains * decays * score).astype(BF16)
                parts.append(
                    dot(rows[h * HEAD_DIM : (h + 1) * HEAD_DIM, lo:hi], weights, NN if forward else NT)
                )
            near.append(jnp.concatenate(parts, axis=0))
        wide = far(0, 256, 512, g3)
        left, right = far(0, 128, 256, g2), far(256, 384, 512, g2)
        if forward:
            near[1] += left
            near[3] += right
            near[2] += wide[:, :128]
            near[3] += wide[:, 128:]
        else:
            near[0] += left
            near[2] += right
            near[0] += wide[:, :128]
            near[1] += wide[:, 128:]
        at = pl.ds(pl.multiple_of(pair * PAIR, PAIR), PAIR)
        for i in range(4):
            out[at, i * 128 : i * 128 + 128] = near[i]
        return carry

    lax.fori_loop(0, NZ, one_pair, 0)


def between(table, upper, lower):
    return [
        jnp.exp(table[h, pl.ds(upper, 1), :] - table[h, pl.ds(lower, 1), :]) for h in range(2)
    ]


def only_if(condition, two):
    return [jnp.where(condition, one, 0.0) for one in two]


def scaled_pair(two, value):
    value = value.astype(F32)
    return jnp.concatenate([value[:HEAD_DIM] * two[0], value[HEAD_DIM:] * two[1]], axis=0)


def running_sums(table, count, scratch):
    for h in range(2):
        total = jnp.zeros((1, STATE), F32)
        for i in range(count):
            table[h, i : i + 1, :] = total
            total = total + scratch[h, i : i + 1, :]
        table[h, count : count + 1, :] = total


def later_sum_kernel(place, got, out, table, scratch):
    z = place[1]
    pieces = got_by_slot(got, z)
    for slot in range(NZ):
        source = (z - slot) & (NZ - 1)
        totals = joined_totals(pieces[slot][5 * PAIR :, :])
        for h in range(2):
            scratch[h, pl.ds(source, 1), :] = totals[h : h + 1]
    running_sums(table, NZ, scratch)
    starts = [between(table, (z - slot) & (NZ - 1), 0) for slot in range(NZ)]
    for b in range(2):
        total = jnp.zeros((PAIR, STATE), F32)
        for slot in range(NZ):
            total += scaled_pair(starts[slot], pieces[slot][(3 + b) * PAIR : (4 + b) * PAIR, :])
        out[b * PAIR : (b + 1) * PAIR, :] = total.astype(BF16)
    whole = jnp.concatenate([table[h, NZ : NZ + 1, :1] for h in range(2)], axis=0)
    out[2 * PAIR :, :] = split_totals(whole)


def state_grad_kernel(place, table, got, *refs):
    x, z = place[0], place[1]
    others, out, x_table, scratch = refs[:3], refs[3], refs[4], refs[5]
    pieces, outs = got_by_slot(got, z), sent_by_slot(out, z)
    for h in range(2):
        scratch[h, pl.ds(x, 1), :] = table[h, NZ : NZ + 1, :]
    for k in range(1, NX):
        source = (x - k) & (NX - 1)
        totals = joined_totals(others[k - 1][2 * PAIR :, :])
        for h in range(2):
            scratch[h, pl.ds(source, 1), :] = totals[h : h + 1]
    running_sums(x_table, NX, scratch)
    later = jnp.zeros((PAIR, STATE), F32)
    for k in range(1, NX):
        source = (x - k) & (NX - 1)
        two = only_if(source > x, between(x_table, source, jnp.minimum(x + 1, source)))
        level = ((source ^ x) > 1).astype(jnp.int32)
        later += scaled_pair(two, rows_at(others[k - 1], level))
    for slot in range(NZ):
        target = (z + slot) & (NZ - 1)
        total = scaled_pair(between(table, NZ, target + 1), later)
        for back in range(NZ):
            source = (z - back) & (NZ - 1)
            two = only_if(source > target, between(table, source, jnp.minimum(target + 1, source)))
            mixed = source ^ target
            level = (mixed > 1).astype(jnp.int32) + (mixed > 3).astype(jnp.int32)
            total += scaled_pair(two, pieces[back][row_block(level), :])
        outs[slot][...] = total.astype(BF16)


def block_sum_kernel(place, table, got, out):
    z = place[1]
    pieces = got_by_slot(got, z)
    total = jnp.zeros((PAIR, STATE), F32)
    for slot in range(NZ):
        source = (z - slot) & (NZ - 1)
        total += scaled_pair(between(table, NZ, source + 1), pieces[slot][...])
    out[...] = total.astype(BF16)


def bucket_kernel(place, table, x_table, got, *refs):
    x, z = place[0], place[1]
    others, out, scratch = refs[:3], refs[3], refs[4]
    pieces, outs = got_by_slot(got, z), sent_by_slot(out, z)
    earlier = [jnp.zeros((PAIR, STATE), F32) for _ in range(2)]
    for k in range(1, NX):
        source = (x - k) & (NX - 1)
        two = between(x_table, x, jnp.minimum(source + 1, x))
        for b in range(2):
            keep = (source < x) & (((source ^ x) > 1) == (b == 1))
            earlier[b] += scaled_pair(only_if(keep, two), others[k - 1][...])
    for slot in range(NZ):
        target = (z + slot) & (NZ - 1)
        for b in range(3):
            scratch[b] = jnp.zeros((PAIR, STATE), F32)
        for back in range(NZ):
            source = (z - back) & (NZ - 1)
            two = only_if(source < target, between(table, target, jnp.minimum(source + 1, target)))
            mixed = source ^ target
            at = (mixed > 1).astype(jnp.int32) + (mixed > 3).astype(jnp.int32)
            scratch[at] = scratch[at] + scaled_pair(two, pieces[back][...])
        for b in range(3):
            outs[slot][b] = scratch[b].astype(BF16)
        start = between(table, target, 0)
        for b in range(2):
            outs[slot][3 + b] = scaled_pair(start, earlier[b]).astype(BF16)


def values_grad_kernel(place, local, write, cum, got, out):
    z = place[1]
    states = got_by_slot(got, z)
    write_rows = write[...]
    for slot in range(NZ):
        pair = (z - slot) & (NZ - 1)
        c = cum[pair]
        rows = dot(states[slot][...], write_rows, NT) * spread(jnp.exp(c[:, TOK - 1 :] - c))
        rows += rows_at(local, pair)
        out[:, pl.ds(pl.multiple_of(pair * PAIR, PAIR), PAIR)] = rows.T.astype(BF16)


def layer_out_kernel(place, local, read, cum, gain, got, out):
    z = place[1]
    buckets = got_by_slot(got, z)
    read_rows = read[...]
    for slot in range(NZ):
        pair = (z - slot) & (NZ - 1)
        decay = jnp.exp(cum[pair])
        rows = rows_at(local, pair)
        for b in range(5):
            rows += dot(buckets[slot][b], read_rows, NT) * spread(gain[LOCAL + b, pair] * decay)
        out[:, pl.ds(pl.multiple_of(pair * PAIR, PAIR), PAIR)] = rows.T.astype(BF16)


def shift(value, axis, apart):
    size = lax.axis_size(axis)
    return lax.ppermute(value, axis, [(i, (i + apart) % size) for i in range(size)])


def exchange(stacked):
    return lax.all_to_all(stacked, "seq_1", split_axis=0, concat_axis=0, tiled=True)


def sent_by_slot(ref, z):
    return [ref.at[(z + slot) & (NZ - 1)] for slot in range(NZ)]


def got_by_slot(ref, z):
    return [ref.at[(z - slot) & (NZ - 1)] for slot in range(NZ)]


def around_x(value):
    return [shift(value, "seq_0", k) for k in range(1, NX)]


def gather_tokens(tokens, sent, deal_out, finish):
    head = lax.axis_index("head")
    y, core = head // 2, head % 2
    half = tokens.shape[0] // 2
    up, down = shift(tokens, "head", 2), shift(tokens, "head", -2)
    up, down, sent = lax.optimization_barrier((up, down, sent))
    far = [shift(up[:half], "head", 2), shift(down[half:], "head", -2)]
    got = deal_out(sent)
    far, got = lax.optimization_barrier((far, got))
    mine = jnp.zeros((4,) + tokens.shape, tokens.dtype)
    at = lambda k: ((y - k) & 3, 0, 0)
    mine = lax.dynamic_update_slice(mine, tokens[None], at(0))
    mine = lax.dynamic_update_slice(mine, up[None], at(1))
    mine = lax.dynamic_update_slice(mine, jnp.concatenate(far, axis=0)[None], at(2))
    mine = lax.dynamic_update_slice(mine, down[None], at(3))
    other = lax.ppermute(mine, "head", [(i, i ^ 1) for i in range(8)])
    values_grad, other = lax.optimization_barrier((finish(got), other))
    first = jnp.where(core == 0, mine, other)
    second = jnp.where(core == 0, other, mine)
    full = jnp.stack([first, second], axis=1).reshape(-1, tokens.shape[1])
    return full, values_grad


def ring_scatter(chunk, axis):
    size = lax.axis_size(axis)
    place = lax.axis_index(axis)
    half = size // 2
    ahead, back = chunk((place + half) % size), chunk((place - half + 1) % size)
    for step in range(half - 1, -1, -1):
        ahead = shift(ahead, axis, 1)
        if step > 0:
            ahead = ahead + chunk((place + step) % size)
        if step < half - 1:
            back = shift(back, axis, -1)
            if step > 0:
                back = back + chunk((place - step) % size)
    total = chunk(place).astype(F32) + ahead.astype(F32) + back.astype(F32)
    return total.astype(BF16)


def per_device(tokens, in_weight, write_proj, read_proj, log_decay, level_gain, out_grad):
    x, z = lax.axis_index("seq_0"), lax.axis_index("seq_1")
    place = jnp.stack([x, z]).astype(jnp.int32)
    both = lax.all_gather(
        jnp.concatenate([write_proj, read_proj], axis=1), "head", axis=0, tiled=True
    )
    write, read = both[:, :STATE], both[:, STATE:]
    weight = lax.all_gather(in_weight, SEQ, axis=0, tiled=True)
    cum = jnp.cumsum(log_decay, axis=1).reshape(NZ, 2, TOK)
    gain = level_gain.reshape(LOCAL + 5, NZ, 2, TOK)

    piece5, piece = shaped((5, PAIR, STATE), BF16), shaped((PAIR, STATE), BF16)
    with_totals = lambda levels: shaped((levels * PAIR + 16, STATE), BF16)
    table_shape = lambda count: shaped((2, count, STATE), F32)
    rows = shaped((NZ * PAIR, TOK), F32)
    natural = shaped((TOK, NZ * PAIR), BF16)

    def local(source, forward, name):
        kernel = lambda *refs: local_kernel(forward, *refs)
        return call(kernel, name, [rows], 0, 5, [pltpu.VMEM((TOK, TOK), F32)])(
            source, read, write, cum, gain
        )[0]

    stacked = lambda item: shaped((NZ,) + item.shape, BF16)
    sent = call(level_grad_kernel, "level_grad", [stacked(with_totals(5))], 1, 4)(
        place, out_grad, read, cum, gain
    )[0]

    def finish(got):
        later, table = call(
            later_sum_kernel,
            "later_sum",
            [with_totals(2), table_shape(16)],
            1,
            1,
            [pltpu.VMEM((2, NZ, STATE), F32)],
        )(place, got)
        grads, x_table = call(
            state_grad_kernel,
            "state_grad",
            [stacked(piece), table_shape(8)],
            1,
            5,
            [pltpu.VMEM((2, NZ, STATE), F32)],
        )(place, table, got, *around_x(later))
        local_grad = local(out_grad, False, "local_bwd")
        return x_table, table, call(values_grad_kernel, "values_grad", [natural], 1, 4)(
            place, local_grad, write, cum, exchange(grads)
        )[0]

    full_tokens, (x_table, table, values_grad) = gather_tokens(tokens, sent, exchange, finish)
    partial = lax.dot_general(
        full_tokens, values_grad, (((0,), (0,)), ((), ())), preferred_element_type=F32
    ).astype(BF16)
    partial, weight = lax.optimization_barrier((partial, weight))
    weight_grad = lax.psum_scatter(partial, "seq_0", scatter_dimension=0, tiled=True)

    values = jnp.dot(full_tokens, weight, preferred_element_type=F32).astype(BF16)
    states = call(state_kernel, "seg_state", [stacked(piece)], 1, 3)(place, values, write, cum)[0]
    got = exchange(states)
    block = call(block_sum_kernel, "block_sum", [piece], 1, 2)(place, table, got)[0]
    buckets = call(
        bucket_kernel, "bucket", [stacked(piece5)], 1, 6, [pltpu.VMEM((3, PAIR, STATE), F32)]
    )(place, table, x_table, got, *around_x(block))[0]
    local_out = local(values, True, "local_fwd")
    layer_out = call(layer_out_kernel, "layer_out", [natural], 1, 5)(
        place, local_out, read, cum, gain, exchange(buckets)
    )[0]
    weight_grad, layer_out = lax.optimization_barrier((weight_grad, layer_out))
    part = STATE
    weight_grad = ring_scatter(
        lambda at: lax.dynamic_slice_in_dim(weight_grad, at * part, part, axis=0), "seq_1"
    )
    return (layer_out, weight_grad)


def solution(mesh):
    split = Mesh(mesh.devices.reshape(NX, NZ, mesh.shape["head"]), ("seq_0", "seq_1", "head"))
    in_specs = (
        P(SEQ_HEAD, None),
        P(SEQ, "head"),
        P(SEQ_HEAD, None),
        P(SEQ_HEAD, None),
        P("head", SEQ),
        P(None, "head", SEQ),
        P(SEQ, "head"),
    )
    out_specs = (P(SEQ, "head"), P(SEQ, "head"))
    return jax.shard_map(
        per_device, mesh=split, in_specs=in_specs, out_specs=out_specs, check_vma=False
    )
```

```python
import jax
import jax.numpy as jnp
from jax import lax
from jax.experimental import pallas as pl
from jax.experimental.pallas import tpu as pltpu
from jax.sharding import Mesh
from jax.sharding import PartitionSpec as P

HEAD_DIM = 64
STATE = 128
TOK = 512
CH = 64
NZ = 8
NX = 4
PAIR = 2 * HEAD_DIM
LOCAL = 4
SEQ = ("seq_0", "seq_1")
SEQ_HEAD = ("seq_0", "seq_1", "head")
F32 = jnp.float32
BF16 = jnp.bfloat16

NT = (((1,), (1,)), ((), ()))
NN = (((1,), (0,)), ((), ()))


def dot(a, b, dims=NN):
    return lax.dot_general(a, b, dims, preferred_element_type=F32)


def spread(rows, each=HEAD_DIM):
    n, t = rows.shape
    return jnp.concatenate([jnp.broadcast_to(rows[i : i + 1], (each, t)) for i in range(n)], axis=0)


def owner_of(slot_base, slot):
    return (slot_base + slot) & (NZ - 1)


def columns(ref, pair):
    return ref[:, pl.ds(pl.multiple_of(pair * PAIR, PAIR), PAIR)]


def row_block(index):
    return pl.ds(pl.multiple_of(index * PAIR, PAIR), PAIR)


def rows_at(ref, index):
    return ref[row_block(index), :]


def vmem():
    return pl.BlockSpec(memory_space=pltpu.VMEM)


def smem():
    return pl.BlockSpec(memory_space=pltpu.SMEM)


def call(kernel, name, outs, n_smem, n_vmem, scratch=(), flops=0):
    return pl.pallas_call(
        kernel,
        name=name,
        out_shape=outs,
        in_specs=[smem()] * n_smem + [vmem()] * n_vmem,
        out_specs=[vmem() for _ in outs],
        scratch_shapes=scratch,
        compiler_params=pltpu.CompilerParams(vmem_limit_bytes=48 << 20),
    )


def shaped(shape, dtype):
    return jax.ShapeDtypeStruct(shape, dtype)


def split_totals(totals):
    wide = jnp.broadcast_to(totals, (2, STATE))
    high = wide.astype(BF16).astype(F32)
    rest = wide - high
    middle = rest.astype(BF16).astype(F32)
    rows = [high, middle, rest - middle, jnp.zeros((10, STATE), F32)]
    return jnp.concatenate(rows, axis=0).astype(BF16)


def joined_totals(rows):
    rows = rows.astype(F32)
    return rows[0:2] + rows[2:4] + rows[4:6]


def level_grad_kernel(place, grad, read, cum, gain, out):
    z = place[1]
    outs = sent_by_slot(out, z)
    read_rows = read[...]
    for slot in range(NZ):
        pair = owner_of(z, slot)
        rows = columns(grad, pair).astype(F32).T
        c = cum[pair]
        decay = jnp.exp(c)
        for b in range(5):
            scaled = (rows * spread(gain[LOCAL + b, pair] * decay)).astype(BF16)
            outs[slot][b * PAIR : (b + 1) * PAIR, :] = dot(scaled, read_rows).astype(BF16)
        outs[slot][5 * PAIR :, :] = split_totals(c[:, TOK - 1 :])


def state_kernel(place, values, write, cum, out):
    z = place[1]
    outs = sent_by_slot(out, z)
    write_rows = write[...]
    for slot in range(NZ):
        pair = owner_of(z, slot)
        rows = columns(values, pair).astype(F32).T
        c = cum[pair]
        scaled = (rows * spread(jnp.exp(c[:, TOK - 1 :] - c))).astype(BF16)
        outs[slot][...] = dot(scaled, write_rows).astype(BF16)


def local_kernel(forward, source, read, write, cum, gain, out, score_ref):
    score_ref[...] = dot(write[...], read[...], NT)
    half = score_ref[...].astype(BF16)
    row_id = lax.broadcasted_iota(jnp.int32, (128, 128), 0)
    col_id = lax.broadcasted_iota(jnp.int32, (128, 128), 1)
    causal = row_id <= col_id
    crosses = (row_id < CH) & (col_id >= CH)

    def one_pair(pair, carry):
        rows = columns(source, pair).T
        rows_f = rows.astype(F32)
        c = cum[pair]
        c_col = jnp.concatenate([c, jnp.zeros((6, TOK), F32)], axis=0).T
        g0, g1, g2, g3 = (gain[level, pair] for level in range(LOCAL))

        def far(lo, mid, hi, g):
            edge = c[:, mid - 1 : mid]
            before = spread(jnp.exp(edge - c[:, lo:mid]))
            after = spread(g[:, mid:hi] * jnp.exp(c[:, mid:hi] - edge))
            block = half[lo:mid, mid:hi]
            if forward:
                return dot((rows_f[:, lo:mid] * before).astype(BF16), block) * after
            return dot((rows_f[:, mid:hi] * after).astype(BF16), block, NT) * before

        near = []
        for i in range(4):
            lo, hi = i * 128, i * 128 + 128
            score = score_ref[lo:hi, lo:hi]
            parts = []
            for h in range(2):
                differ = c[h : h + 1, lo:hi] - c_col[lo:hi, h : h + 1]
                decays = jnp.exp(jnp.where(causal, differ, -1e30))
                gains = jnp.where(crosses, g1[h : h + 1, lo:hi], g0[h : h + 1, lo:hi])
                weights = (gains * decays * score).astype(BF16)
                parts.append(
                    dot(rows[h * HEAD_DIM : (h + 1) * HEAD_DIM, lo:hi], weights, NN if forward else NT)
                )
            near.append(jnp.concatenate(parts, axis=0))
        wide = far(0, 256, 512, g3)
        left, right = far(0, 128, 256, g2), far(256, 384, 512, g2)
        if forward:
            near[1] += left
            near[3] += right
            near[2] += wide[:, :128]
            near[3] += wide[:, 128:]
        else:
            near[0] += left
            near[2] += right
            near[0] += wide[:, :128]
            near[1] += wide[:, 128:]
        at = pl.ds(pl.multiple_of(pair * PAIR, PAIR), PAIR)
        for i in range(4):
            out[at, i * 128 : i * 128 + 128] = near[i]
        return carry

    lax.fori_loop(0, NZ, one_pair, 0)


def between(table, upper, lower):
    return [
        jnp.exp(table[h, pl.ds(upper, 1), :] - table[h, pl.ds(lower, 1), :]) for h in range(2)
    ]


def only_if(condition, two):
    return [jnp.where(condition, one, 0.0) for one in two]


def scaled_pair(two, value):
    value = value.astype(F32)
    return jnp.concatenate([value[:HEAD_DIM] * two[0], value[HEAD_DIM:] * two[1]], axis=0)


def running_sums(table, count, scratch):
    for h in range(2):
        total = jnp.zeros((1, STATE), F32)
        for i in range(count):
            table[h, i : i + 1, :] = total
            total = total + scratch[h, i : i + 1, :]
        table[h, count : count + 1, :] = total


def later_sum_kernel(place, got, out, table, scratch):
    z = place[1]
    pieces = got_by_slot(got, z)
    for slot in range(NZ):
        source = (z - slot) & (NZ - 1)
        totals = joined_totals(pieces[slot][5 * PAIR :, :])
        for h in range(2):
            scratch[h, pl.ds(source, 1), :] = totals[h : h + 1]
    running_sums(table, NZ, scratch)
    starts = [between(table, (z - slot) & (NZ - 1), 0) for slot in range(NZ)]
    for b in range(2):
        total = jnp.zeros((PAIR, STATE), F32)
        for slot in range(NZ):
            total += scaled_pair(starts[slot], pieces[slot][(3 + b) * PAIR : (4 + b) * PAIR, :])
        out[b * PAIR : (b + 1) * PAIR, :] = total.astype(BF16)
    whole = jnp.concatenate([table[h, NZ : NZ + 1, :1] for h in range(2)], axis=0)
    out[2 * PAIR :, :] = split_totals(whole)


def state_grad_kernel(place, table, got, *refs):
    x, z = place[0], place[1]
    others, out, x_table, scratch = refs[:3], refs[3], refs[4], refs[5]
    pieces, outs = got_by_slot(got, z), sent_by_slot(out, z)
    for h in range(2):
        scratch[h, pl.ds(x, 1), :] = table[h, NZ : NZ + 1, :]
    for k in range(1, NX):
        source = (x - k) & (NX - 1)
        totals = joined_totals(others[k - 1][2 * PAIR :, :])
        for h in range(2):
            scratch[h, pl.ds(source, 1), :] = totals[h : h + 1]
    running_sums(x_table, NX, scratch)
    later = jnp.zeros((PAIR, STATE), F32)
    for k in range(1, NX):
        source = (x - k) & (NX - 1)
        two = only_if(source > x, between(x_table, source, jnp.minimum(x + 1, source)))
        level = ((source ^ x) > 1).astype(jnp.int32)
        later += scaled_pair(two, rows_at(others[k - 1], level))
    for slot in range(NZ):
        target = (z + slot) & (NZ - 1)
        total = scaled_pair(between(table, NZ, target + 1), later)
        for back in range(NZ):
            source = (z - back) & (NZ - 1)
            two = only_if(source > target, between(table, source, jnp.minimum(target + 1, source)))
            mixed = source ^ target
            level = (mixed > 1).astype(jnp.int32) + (mixed > 3).astype(jnp.int32)
            total += scaled_pair(two, pieces[back][row_block(level), :])
        outs[slot][...] = total.astype(BF16)


def block_sum_kernel(place, table, got, out):
    z = place[1]
    pieces = got_by_slot(got, z)
    total = jnp.zeros((PAIR, STATE), F32)
    for slot in range(NZ):
        source = (z - slot) & (NZ - 1)
        total += scaled_pair(between(table, NZ, source + 1), pieces[slot][...])
    out[...] = total.astype(BF16)


def bucket_kernel(place, table, x_table, got, *refs):
    x, z = place[0], place[1]
    others, out, scratch = refs[:3], refs[3], refs[4]
    pieces, outs = got_by_slot(got, z), sent_by_slot(out, z)
    earlier = [jnp.zeros((PAIR, STATE), F32) for _ in range(2)]
    for k in range(1, NX):
        source = (x - k) & (NX - 1)
        two = between(x_table, x, jnp.minimum(source + 1, x))
        for b in range(2):
            keep = (source < x) & (((source ^ x) > 1) == (b == 1))
            earlier[b] += scaled_pair(only_if(keep, two), others[k - 1][...])
    for slot in range(NZ):
        target = (z + slot) & (NZ - 1)
        for b in range(3):
            scratch[b] = jnp.zeros((PAIR, STATE), F32)
        for back in range(NZ):
            source = (z - back) & (NZ - 1)
            two = only_if(source < target, between(table, target, jnp.minimum(source + 1, target)))
            mixed = source ^ target
            at = (mixed > 1).astype(jnp.int32) + (mixed > 3).astype(jnp.int32)
            scratch[at] = scratch[at] + scaled_pair(two, pieces[back][...])
        for b in range(3):
            outs[slot][b] = scratch[b].astype(BF16)
        start = between(table, target, 0)
        for b in range(2):
            outs[slot][3 + b] = scaled_pair(start, earlier[b]).astype(BF16)


def values_grad_kernel(place, local, write, cum, got, out):
    z = place[1]
    states = got_by_slot(got, z)
    write_rows = write[...]
    for slot in range(NZ):
        pair = (z - slot) & (NZ - 1)
        c = cum[pair]
        rows = dot(states[slot][...], write_rows, NT) * spread(jnp.exp(c[:, TOK - 1 :] - c))
        rows += rows_at(local, pair)
        out[:, pl.ds(pl.multiple_of(pair * PAIR, PAIR), PAIR)] = rows.T.astype(BF16)


def layer_out_kernel(place, local, read, cum, gain, got, out):
    z = place[1]
    buckets = got_by_slot(got, z)
    read_rows = read[...]
    for slot in range(NZ):
        pair = (z - slot) & (NZ - 1)
        decay = jnp.exp(cum[pair])
        rows = rows_at(local, pair)
        for b in range(5):
            rows += dot(buckets[slot][b], read_rows, NT) * spread(gain[LOCAL + b, pair] * decay)
        out[:, pl.ds(pl.multiple_of(pair * PAIR, PAIR), PAIR)] = rows.T.astype(BF16)


def shift(value, axis, apart):
    size = lax.axis_size(axis)
    return lax.ppermute(value, axis, [(i, (i + apart) % size) for i in range(size)])


def exchange(stacked):
    return lax.all_to_all(stacked, "seq_1", split_axis=0, concat_axis=0, tiled=True)


def sent_by_slot(ref, z):
    return [ref.at[(z + slot) & (NZ - 1)] for slot in range(NZ)]


def got_by_slot(ref, z):
    return [ref.at[(z - slot) & (NZ - 1)] for slot in range(NZ)]


def around_x(value):
    return [shift(value, "seq_0", k) for k in range(1, NX)]


def gather_tokens(tokens, sent, deal_out, finish):
    head = lax.axis_index("head")
    y, core = head // 2, head % 2
    half = tokens.shape[0] // 2
    up, down = shift(tokens, "head", 2), shift(tokens, "head", -2)
    up, down, sent = lax.optimization_barrier((up, down, sent))
    far = [shift(up[:half], "head", 2), shift(down[half:], "head", -2)]
    got = deal_out(sent)
    far, got = lax.optimization_barrier((far, got))
    pieces = [tokens, up, jnp.concatenate(far, axis=0), down]
    mine = jnp.zeros((4,) + tokens.shape, tokens.dtype)
    for k, piece in enumerate(pieces):
        mine = lax.dynamic_update_slice(mine, piece[None], ((y - k) & 3, 0, 0))
    other = lax.ppermute(mine, "head", [(i, i ^ 1) for i in range(8)])
    values_grad = finish(got)
    full = jnp.zeros((4, 2) + tokens.shape, tokens.dtype)
    full = lax.dynamic_update_slice(full, mine[:, None], (0, core, 0, 0))
    full = lax.dynamic_update_slice(full, other[:, None], (0, 1 - core, 0, 0))
    return full.reshape(-1, tokens.shape[1]), values_grad


def ring_scatter(chunk, axis):
    size = lax.axis_size(axis)
    place = lax.axis_index(axis)
    half = size // 2
    ahead, back = chunk((place + half) % size), chunk((place - half + 1) % size)
    for step in range(half - 1, -1, -1):
        ahead = shift(ahead, axis, 1)
        if step > 0:
            ahead = ahead + chunk((place + step) % size)
        if step < half - 1:
            back = shift(back, axis, -1)
            if step > 0:
                back = back + chunk((place - step) % size)
    total = chunk(place).astype(F32) + ahead.astype(F32) + back.astype(F32)
    return total.astype(BF16)


def per_device(tokens, in_weight, write_proj, read_proj, log_decay, level_gain, out_grad):
    x, z = lax.axis_index("seq_0"), lax.axis_index("seq_1")
    place = jnp.stack([x, z]).astype(jnp.int32)
    both = lax.all_gather(
        jnp.concatenate([write_proj, read_proj], axis=1), "head", axis=0, tiled=True
    )
    write, read = both[:, :STATE], both[:, STATE:]
    weight = lax.all_gather(in_weight, SEQ, axis=0, tiled=True)
    cum = jnp.cumsum(log_decay, axis=1).reshape(NZ, 2, TOK)
    gain = level_gain.reshape(LOCAL + 5, NZ, 2, TOK)

    piece5, piece = shaped((5, PAIR, STATE), BF16), shaped((PAIR, STATE), BF16)
    with_totals = lambda levels: shaped((levels * PAIR + 16, STATE), BF16)
    table_shape = lambda count: shaped((2, count, STATE), F32)
    rows = shaped((NZ * PAIR, TOK), F32)
    natural = shaped((TOK, NZ * PAIR), BF16)

    def local(source, forward, name):
        kernel = lambda *refs: local_kernel(forward, *refs)
        return call(kernel, name, [rows], 0, 5, [pltpu.VMEM((TOK, TOK), F32)])(
            source, read, write, cum, gain
        )[0]

    stacked = lambda item: shaped((NZ,) + item.shape, BF16)
    sent = call(level_grad_kernel, "level_grad", [stacked(with_totals(5))], 1, 4)(
        place, out_grad, read, cum, gain
    )[0]

    def finish(got):
        later, table = call(
            later_sum_kernel,
            "later_sum",
            [with_totals(2), table_shape(16)],
            1,
            1,
            [pltpu.VMEM((2, NZ, STATE), F32)],
        )(place, got)
        grads, x_table = call(
            state_grad_kernel,
            "state_grad",
            [stacked(piece), table_shape(8)],
            1,
            5,
            [pltpu.VMEM((2, NZ, STATE), F32)],
        )(place, table, got, *around_x(later))
        local_grad = local(out_grad, False, "local_bwd")
        return x_table, table, call(values_grad_kernel, "values_grad", [natural], 1, 4)(
            place, local_grad, write, cum, exchange(grads)
        )[0]

    full_tokens, (x_table, table, values_grad) = gather_tokens(tokens, sent, exchange, finish)
    partial = lax.dot_general(
        full_tokens, values_grad, (((0,), (0,)), ((), ())), preferred_element_type=F32
    ).astype(BF16)
    partial, weight = lax.optimization_barrier((partial, weight))
    weight_grad = lax.psum_scatter(partial, "seq_0", scatter_dimension=0, tiled=True)

    values = jnp.dot(full_tokens, weight, preferred_element_type=F32).astype(BF16)
    states = call(state_kernel, "seg_state", [stacked(piece)], 1, 3)(place, values, write, cum)[0]
    got = exchange(states)
    block = call(block_sum_kernel, "block_sum", [piece], 1, 2)(place, table, got)[0]
    buckets = call(
        bucket_kernel, "bucket", [stacked(piece5)], 1, 6, [pltpu.VMEM((3, PAIR, STATE), F32)]
    )(place, table, x_table, got, *around_x(block))[0]
    local_out = local(values, True, "local_fwd")
    layer_out = call(layer_out_kernel, "layer_out", [natural], 1, 5)(
        place, local_out, read, cum, gain, exchange(buckets)
    )[0]
    weight_grad, layer_out = lax.optimization_barrier((weight_grad, layer_out))
    part = STATE
    weight_grad = ring_scatter(
        lambda at: lax.dynamic_slice_in_dim(weight_grad, at * part, part, axis=0), "seq_1"
    )
    return (layer_out, weight_grad)


def solution(mesh):
    split = Mesh(mesh.devices.reshape(NX, NZ, mesh.shape["head"]), ("seq_0", "seq_1", "head"))
    in_specs = (
        P(SEQ_HEAD, None),
        P(SEQ, "head"),
        P(SEQ_HEAD, None),
        P(SEQ_HEAD, None),
        P("head", SEQ),
        P(None, "head", SEQ),
        P(SEQ, "head"),
    )
    out_specs = (P(SEQ, "head"), P(SEQ, "head"))
    return jax.shard_map(
        per_device, mesh=split, in_specs=in_specs, out_specs=out_specs, check_vma=False
    )
```

```python
import jax
import jax.numpy as jnp
from jax import lax
from jax.experimental import pallas as pl
from jax.experimental.pallas import tpu as pltpu
from jax.sharding import Mesh
from jax.sharding import PartitionSpec as P

HEAD_DIM = 64
STATE = 128
TOK = 512
CH = 64
NZ = 8
NX = 4
PAIR = 2 * HEAD_DIM
LOCAL = 4
SEQ = ("seq_0", "seq_1")
SEQ_HEAD = ("seq_0", "seq_1", "head")
F32 = jnp.float32
BF16 = jnp.bfloat16

NT = (((1,), (1,)), ((), ()))
NN = (((1,), (0,)), ((), ()))


def dot(a, b, dims=NN):
    return lax.dot_general(a, b, dims, preferred_element_type=F32)


def spread(rows, each=HEAD_DIM):
    n, t = rows.shape
    return jnp.concatenate([jnp.broadcast_to(rows[i : i + 1], (each, t)) for i in range(n)], axis=0)


def owner_of(slot_base, slot):
    return (slot_base + slot) & (NZ - 1)


def columns(ref, pair):
    return ref[:, pl.ds(pl.multiple_of(pair * PAIR, PAIR), PAIR)]


def row_block(index):
    return pl.ds(pl.multiple_of(index * PAIR, PAIR), PAIR)


def rows_at(ref, index):
    return ref[row_block(index), :]


def vmem():
    return pl.BlockSpec(memory_space=pltpu.VMEM)


def smem():
    return pl.BlockSpec(memory_space=pltpu.SMEM)


def call(kernel, name, outs, n_smem, n_vmem, scratch=(), flops=0):
    return pl.pallas_call(
        kernel,
        name=name,
        out_shape=outs,
        in_specs=[smem()] * n_smem + [vmem()] * n_vmem,
        out_specs=[vmem() for _ in outs],
        scratch_shapes=scratch,
        compiler_params=pltpu.CompilerParams(vmem_limit_bytes=48 << 20),
    )


def shaped(shape, dtype):
    return jax.ShapeDtypeStruct(shape, dtype)


def split_totals(totals):
    wide = jnp.broadcast_to(totals, (2, STATE))
    high = wide.astype(BF16).astype(F32)
    rest = wide - high
    middle = rest.astype(BF16).astype(F32)
    rows = [high, middle, rest - middle, jnp.zeros((10, STATE), F32)]
    return jnp.concatenate(rows, axis=0).astype(BF16)


def joined_totals(rows):
    rows = rows.astype(F32)
    return rows[0:2] + rows[2:4] + rows[4:6]


def level_grad_kernel(place, grad, read, cum, gain, out):
    z = place[1]
    outs = sent_by_slot(out, z)
    read_rows = read[...]
    for slot in range(NZ):
        pair = owner_of(z, slot)
        rows = columns(grad, pair).astype(F32).T
        c = cum[pair]
        decay = jnp.exp(c)
        for b in range(5):
            scaled = (rows * spread(gain[LOCAL + b, pair] * decay)).astype(BF16)
            outs[slot][b * PAIR : (b + 1) * PAIR, :] = dot(scaled, read_rows).astype(BF16)
        outs[slot][5 * PAIR :, :] = split_totals(c[:, TOK - 1 :])


def state_kernel(place, values, write, cum, out):
    z = place[1]
    outs = sent_by_slot(out, z)
    write_rows = write[...]
    for slot in range(NZ):
        pair = owner_of(z, slot)
        rows = columns(values, pair).astype(F32).T
        c = cum[pair]
        scaled = (rows * spread(jnp.exp(c[:, TOK - 1 :] - c))).astype(BF16)
        outs[slot][...] = dot(scaled, write_rows).astype(BF16)


def local_kernel(forward, source, read, write, cum, gain, out, score_ref):
    score_ref[...] = dot(write[...], read[...], NT)
    half = score_ref[...].astype(BF16)
    row_id = lax.broadcasted_iota(jnp.int32, (128, 128), 0)
    col_id = lax.broadcasted_iota(jnp.int32, (128, 128), 1)
    causal = row_id <= col_id
    crosses = (row_id < CH) & (col_id >= CH)

    def one_pair(pair, carry):
        rows = columns(source, pair).T
        rows_f = rows.astype(F32)
        c = cum[pair]
        c_col = jnp.concatenate([c, jnp.zeros((6, TOK), F32)], axis=0).T
        g0, g1, g2, g3 = (gain[level, pair] for level in range(LOCAL))

        def far(lo, mid, hi, g):
            edge = c[:, mid - 1 : mid]
            before = spread(jnp.exp(edge - c[:, lo:mid]))
            after = spread(g[:, mid:hi] * jnp.exp(c[:, mid:hi] - edge))
            block = half[lo:mid, mid:hi]
            if forward:
                return dot((rows_f[:, lo:mid] * before).astype(BF16), block) * after
            return dot((rows_f[:, mid:hi] * after).astype(BF16), block, NT) * before

        near = []
        for i in range(4):
            lo, hi = i * 128, i * 128 + 128
            score = score_ref[lo:hi, lo:hi]
            parts = []
            for h in range(2):
                differ = c[h : h + 1, lo:hi] - c_col[lo:hi, h : h + 1]
                decays = jnp.exp(jnp.where(causal, differ, -1e30))
                gains = jnp.where(crosses, g1[h : h + 1, lo:hi], g0[h : h + 1, lo:hi])
                weights = (gains * decays * score).astype(BF16)
                parts.append(
                    dot(rows[h * HEAD_DIM : (h + 1) * HEAD_DIM, lo:hi], weights, NN if forward else NT)
                )
            near.append(jnp.concatenate(parts, axis=0))
        wide = far(0, 256, 512, g3)
        left, right = far(0, 128, 256, g2), far(256, 384, 512, g2)
        if forward:
            near[1] += left
            near[3] += right
            near[2] += wide[:, :128]
            near[3] += wide[:, 128:]
        else:
            near[0] += left
            near[2] += right
            near[0] += wide[:, :128]
            near[1] += wide[:, 128:]
        at = pl.ds(pl.multiple_of(pair * PAIR, PAIR), PAIR)
        for i in range(4):
            out[at, i * 128 : i * 128 + 128] = near[i]
        return carry

    lax.fori_loop(0, NZ, one_pair, 0)


def between(table, upper, lower):
    return [
        jnp.exp(table[h, pl.ds(upper, 1), :] - table[h, pl.ds(lower, 1), :]) for h in range(2)
    ]


def only_if(condition, two):
    return [jnp.where(condition, one, 0.0) for one in two]


def scaled_pair(two, value):
    value = value.astype(F32)
    return jnp.concatenate([value[:HEAD_DIM] * two[0], value[HEAD_DIM:] * two[1]], axis=0)


def running_sums(table, count, scratch):
    for h in range(2):
        total = jnp.zeros((1, STATE), F32)
        for i in range(count):
            table[h, i : i + 1, :] = total
            total = total + scratch[h, i : i + 1, :]
        table[h, count : count + 1, :] = total


def later_sum_kernel(place, got, out, table, scratch):
    z = place[1]
    pieces = got_by_slot(got, z)
    for slot in range(NZ):
        source = (z - slot) & (NZ - 1)
        totals = joined_totals(pieces[slot][5 * PAIR :, :])
        for h in range(2):
            scratch[h, pl.ds(source, 1), :] = totals[h : h + 1]
    running_sums(table, NZ, scratch)
    starts = [between(table, (z - slot) & (NZ - 1), 0) for slot in range(NZ)]
    for b in range(2):
        total = jnp.zeros((PAIR, STATE), F32)
        for slot in range(NZ):
            total += scaled_pair(starts[slot], pieces[slot][(3 + b) * PAIR : (4 + b) * PAIR, :])
        out[b * PAIR : (b + 1) * PAIR, :] = total.astype(BF16)
    whole = jnp.concatenate([table[h, NZ : NZ + 1, :1] for h in range(2)], axis=0)
    out[2 * PAIR :, :] = split_totals(whole)


def state_grad_kernel(place, table, got, *refs):
    x, z = place[0], place[1]
    others, out, x_table, scratch = refs[:3], refs[3], refs[4], refs[5]
    pieces, outs = got_by_slot(got, z), sent_by_slot(out, z)
    for h in range(2):
        scratch[h, pl.ds(x, 1), :] = table[h, NZ : NZ + 1, :]
    for k in range(1, NX):
        source = (x - k) & (NX - 1)
        totals = joined_totals(others[k - 1][2 * PAIR :, :])
        for h in range(2):
            scratch[h, pl.ds(source, 1), :] = totals[h : h + 1]
    running_sums(x_table, NX, scratch)
    later = jnp.zeros((PAIR, STATE), F32)
    for k in range(1, NX):
        source = (x - k) & (NX - 1)
        two = only_if(source > x, between(x_table, source, jnp.minimum(x + 1, source)))
        level = ((source ^ x) > 1).astype(jnp.int32)
        later += scaled_pair(two, rows_at(others[k - 1], level))
    for slot in range(NZ):
        target = (z + slot) & (NZ - 1)
        total = scaled_pair(between(table, NZ, target + 1), later)
        for back in range(NZ):
            source = (z - back) & (NZ - 1)
            two = only_if(source > target, between(table, source, jnp.minimum(target + 1, source)))
            mixed = source ^ target
            level = (mixed > 1).astype(jnp.int32) + (mixed > 3).astype(jnp.int32)
            total += scaled_pair(two, pieces[back][row_block(level), :])
        outs[slot][...] = total.astype(BF16)


def block_sum_kernel(place, table, got, out):
    z = place[1]
    pieces = got_by_slot(got, z)
    total = jnp.zeros((PAIR, STATE), F32)
    for slot in range(NZ):
        source = (z - slot) & (NZ - 1)
        total += scaled_pair(between(table, NZ, source + 1), pieces[slot][...])
    out[...] = total.astype(BF16)


def bucket_kernel(place, table, x_table, got, *refs):
    x, z = place[0], place[1]
    others, out, scratch = refs[:3], refs[3], refs[4]
    pieces, outs = got_by_slot(got, z), sent_by_slot(out, z)
    earlier = [jnp.zeros((PAIR, STATE), F32) for _ in range(2)]
    for k in range(1, NX):
        source = (x - k) & (NX - 1)
        two = between(x_table, x, jnp.minimum(source + 1, x))
        for b in range(2):
            keep = (source < x) & (((source ^ x) > 1) == (b == 1))
            earlier[b] += scaled_pair(only_if(keep, two), others[k - 1][...])
    for slot in range(NZ):
        target = (z + slot) & (NZ - 1)
        for b in range(3):
            scratch[b] = jnp.zeros((PAIR, STATE), F32)
        for back in range(NZ):
            source = (z - back) & (NZ - 1)
            two = only_if(source < target, between(table, target, jnp.minimum(source + 1, target)))
            mixed = source ^ target
            at = (mixed > 1).astype(jnp.int32) + (mixed > 3).astype(jnp.int32)
            scratch[at] = scratch[at] + scaled_pair(two, pieces[back][...])
        for b in range(3):
            outs[slot][b] = scratch[b].astype(BF16)
        start = between(table, target, 0)
        for b in range(2):
            outs[slot][3 + b] = scaled_pair(start, earlier[b]).astype(BF16)


def values_grad_kernel(place, local, write, cum, got, out):
    z = place[1]
    states = got_by_slot(got, z)
    write_rows = write[...]
    for slot in range(NZ):
        pair = (z - slot) & (NZ - 1)
        c = cum[pair]
        rows = dot(states[slot][...], write_rows, NT) * spread(jnp.exp(c[:, TOK - 1 :] - c))
        rows += rows_at(local, pair)
        out[:, pl.ds(pl.multiple_of(pair * PAIR, PAIR), PAIR)] = rows.T.astype(BF16)


def layer_out_kernel(place, local, read, cum, gain, got, out):
    z = place[1]
    buckets = got_by_slot(got, z)
    read_rows = read[...]
    for slot in range(NZ):
        pair = (z - slot) & (NZ - 1)
        decay = jnp.exp(cum[pair])
        rows = rows_at(local, pair)
        for b in range(5):
            rows += dot(buckets[slot][b], read_rows, NT) * spread(gain[LOCAL + b, pair] * decay)
        out[:, pl.ds(pl.multiple_of(pair * PAIR, PAIR), PAIR)] = rows.T.astype(BF16)


def shift(value, axis, apart):
    size = lax.axis_size(axis)
    return lax.ppermute(value, axis, [(i, (i + apart) % size) for i in range(size)])


def exchange(stacked):
    return lax.all_to_all(stacked, "seq_1", split_axis=0, concat_axis=0, tiled=True)


def sent_by_slot(ref, z):
    return [ref.at[(z + slot) & (NZ - 1)] for slot in range(NZ)]


def got_by_slot(ref, z):
    return [ref.at[(z - slot) & (NZ - 1)] for slot in range(NZ)]


def around_x(value):
    return [shift(value, "seq_0", k) for k in range(1, NX)]


def gather_tokens(tokens, sent, deal_out, finish):
    head = lax.axis_index("head")
    y, core = head // 2, head % 2
    half = tokens.shape[0] // 2
    up, down = shift(tokens, "head", 2), shift(tokens, "head", -2)
    up, down, sent = lax.optimization_barrier((up, down, sent))
    far = [shift(up[:half], "head", 2), shift(down[half:], "head", -2)]
    got = deal_out(sent)
    far, got = lax.optimization_barrier((far, got))
    pieces = [tokens, up, jnp.concatenate(far, axis=0), down]
    mine = jnp.zeros((4,) + tokens.shape, tokens.dtype)
    for k, piece in enumerate(pieces):
        mine = lax.dynamic_update_slice(mine, piece[None], ((y - k) & 3, 0, 0))
    other = lax.ppermute(mine, "head", [(i, i ^ 1) for i in range(8)])
    values_grad = finish(got)
    full = jnp.zeros((4, 2) + tokens.shape, tokens.dtype)
    full = lax.dynamic_update_slice(full, mine[:, None], (0, core, 0, 0))
    full = lax.dynamic_update_slice(full, other[:, None], (0, 1 - core, 0, 0))
    return full.reshape(-1, tokens.shape[1]), values_grad


def ring_scatter(chunk, axis):
    size = lax.axis_size(axis)
    place = lax.axis_index(axis)
    half = size // 2
    ahead, back = chunk((place + half) % size), chunk((place - half + 1) % size)
    for step in range(half - 1, -1, -1):
        ahead = shift(ahead, axis, 1)
        if step > 0:
            ahead = ahead + chunk((place + step) % size)
        if step < half - 1:
            back = shift(back, axis, -1)
            if step > 0:
                back = back + chunk((place - step) % size)
    total = chunk(place).astype(F32) + ahead.astype(F32) + back.astype(F32)
    return total.astype(BF16)


def per_device(tokens, in_weight, write_proj, read_proj, log_decay, level_gain, out_grad):
    x, z = lax.axis_index("seq_0"), lax.axis_index("seq_1")
    place = jnp.stack([x, z]).astype(jnp.int32)
    both = lax.all_gather(
        jnp.concatenate([write_proj, read_proj], axis=1), "head", axis=0, tiled=True
    )
    both, tokens = lax.optimization_barrier((both, tokens))
    write, read = both[:, :STATE], both[:, STATE:]
    weight = lax.all_gather(in_weight, SEQ, axis=0, tiled=True)
    cum = jnp.cumsum(log_decay, axis=1).reshape(NZ, 2, TOK)
    gain = level_gain.reshape(LOCAL + 5, NZ, 2, TOK)

    piece5, piece = shaped((5, PAIR, STATE), BF16), shaped((PAIR, STATE), BF16)
    with_totals = lambda levels: shaped((levels * PAIR + 16, STATE), BF16)
    table_shape = lambda count: shaped((2, count, STATE), F32)
    rows = shaped((NZ * PAIR, TOK), F32)
    natural = shaped((TOK, NZ * PAIR), BF16)

    def local(source, forward, name):
        kernel = lambda *refs: local_kernel(forward, *refs)
        return call(kernel, name, [rows], 0, 5, [pltpu.VMEM((TOK, TOK), F32)])(
            source, read, write, cum, gain
        )[0]

    stacked = lambda item: shaped((NZ,) + item.shape, BF16)
    sent = call(level_grad_kernel, "level_grad", [stacked(with_totals(5))], 1, 4)(
        place, out_grad, read, cum, gain
    )[0]

    def finish(got):
        later, table = call(
            later_sum_kernel,
            "later_sum",
            [with_totals(2), table_shape(16)],
            1,
            1,
            [pltpu.VMEM((2, NZ, STATE), F32)],
        )(place, got)
        grads, x_table = call(
            state_grad_kernel,
            "state_grad",
            [stacked(piece), table_shape(8)],
            1,
            5,
            [pltpu.VMEM((2, NZ, STATE), F32)],
        )(place, table, got, *around_x(later))
        local_grad = local(out_grad, False, "local_bwd")
        return x_table, table, call(values_grad_kernel, "values_grad", [natural], 1, 4)(
            place, local_grad, write, cum, exchange(grads)
        )[0]

    full_tokens, (x_table, table, values_grad) = gather_tokens(tokens, sent, exchange, finish)
    partial = lax.dot_general(
        full_tokens, values_grad, (((0,), (0,)), ((), ())), preferred_element_type=F32
    ).astype(BF16)
    partial, weight = lax.optimization_barrier((partial, weight))
    weight_grad = lax.psum_scatter(partial, "seq_0", scatter_dimension=0, tiled=True)

    values = jnp.dot(full_tokens, weight, preferred_element_type=F32).astype(BF16)
    states = call(state_kernel, "seg_state", [stacked(piece)], 1, 3)(place, values, write, cum)[0]
    got = exchange(states)
    block = call(block_sum_kernel, "block_sum", [piece], 1, 2)(place, table, got)[0]
    buckets = call(
        bucket_kernel, "bucket", [stacked(piece5)], 1, 6, [pltpu.VMEM((3, PAIR, STATE), F32)]
    )(place, table, x_table, got, *around_x(block))[0]
    local_out = local(values, True, "local_fwd")
    layer_out = call(layer_out_kernel, "layer_out", [natural], 1, 5)(
        place, local_out, read, cum, gain, exchange(buckets)
    )[0]
    weight_grad, layer_out = lax.optimization_barrier((weight_grad, layer_out))
    part = STATE
    weight_grad = ring_scatter(
        lambda at: lax.dynamic_slice_in_dim(weight_grad, at * part, part, axis=0), "seq_1"
    )
    return (layer_out, weight_grad)


def solution(mesh):
    split = Mesh(mesh.devices.reshape(NX, NZ, mesh.shape["head"]), ("seq_0", "seq_1", "head"))
    in_specs = (
        P(SEQ_HEAD, None),
        P(SEQ, "head"),
        P(SEQ_HEAD, None),
        P(SEQ_HEAD, None),
        P("head", SEQ),
        P(None, "head", SEQ),
        P(SEQ, "head"),
    )
    out_specs = (P(SEQ, "head"), P(SEQ, "head"))
    return jax.shard_map(
        per_device, mesh=split, in_specs=in_specs, out_specs=out_specs, check_vma=False
    )
```
